32 devices in a mesh: scan: 16 (over z, x, core), mode: 2 (over y).
Axes of the slice: x: 2, y: 2, z: 4, core: 2. Of those that a mesh axis runs over, the one named last changes fastest.
Arguments:
- object_field: float32 [2, 4096, 384], P(None, 'scan'), may hold values from -3 to 3, as said below
- eigen_probes: float32 [2, 2, 256, 256], P('mode'), may hold values from -2.1 to 2.1
- coeffs: float32 [64, 2, 2], P(('scan', 'mode')), may hold values from -4 to 4
- intensities: float32 [64, 256, 256], P(('scan', 'mode')), may hold values from 0.05 to 1
- positions: int32 [64, 2], P(('scan', 'mode')), may hold values from 0 to 3840, as said below
Outputs:
- object_new: float32 [2, 4096, 384], P(None, 'scan')
- probes_new: float32 [2, 2, 256, 256], P('mode')
- coeffs_new: float32 [64, 2, 2], P(('scan', 'mode'))
The draws below stay inside these ranges and needn't reach their ends.
Inputs may be any that keep to these rules, and one draw needn't show every extreme that they name: Pattern j belongs to tile t = j // 4: t * 256 <= positions[j,0] < t * 256 + 256, and positions[j,0] <= 3840; in every tile but the last some pattern has positions[j,0] = t * 256 + 255. positions[j,1] <= 128, reached in every tile. `object_field`: each pixel's magnitude lies between 0.3 and 3.
All inputs are finite; a program needn't handle non-finite values.
Results may differ from the reference program's by a relative error of at most 0.0003.
Values sent between devices are 32-bit elements; how exact they have to be, the bound alone decides.
A program may use at most 128 MiB of HBM per device.

```python
import math
import jax
import jax.numpy as jnp
from jax import lax

N = 256
MODES = 2
OBJ_COLS = 384
PAT_TILE = 4
PATTERNS = 64
ROWS = 4096


def draw_object_field(key, part):
    key_amplitude, key_phase = jax.random.split(jax.random.fold_in(key, 11), 2)
    height = jnp.arange(ROWS, dtype=jnp.float32)[:, None] / ROWS
    rising = 0.6 + 1.2 * height
    rough = jax.random.uniform(key_amplitude, (ROWS, OBJ_COLS), jnp.float32, 0.6, 1.4)
    phase = jax.random.uniform(key_phase, (ROWS, OBJ_COLS), jnp.float32, -math.pi, math.pi)
    amplitude = rising * rough
    return jnp.stack([amplitude * jnp.cos(phase), amplitude * jnp.sin(phase)]).astype(jnp.float32)


def draw_positions(key, part):
    key_rows, key_columns = jax.random.split(jax.random.fold_in(key, 23), 2)
    pattern = jnp.arange(PATTERNS, dtype=jnp.int32)
    tile = pattern // PAT_TILE
    within = pattern % PAT_TILE
    offset = jax.random.randint(key_rows, (PATTERNS,), 0, N, dtype=jnp.int32)
    offset = jnp.where(within == 1, N - 1, jnp.where(within == 0, 0, offset))
    first = jnp.minimum(tile * N + offset, ROWS - N)
    second = jax.random.randint(key_columns, (PATTERNS,), 0, OBJ_COLS - N + 1, dtype=jnp.int32)
    second = jnp.where(within == 0, OBJ_COLS - N, second)
    return jnp.stack([first, second], axis=1).astype(jnp.int32)


def level_of(stream_key, shape, cuts, least, high):
    factor_of, own = 1.0, jax.random.fold_in(stream_key, 6)
    for dim, shards_of in cuts:
        draws = jnp.exp(jax.random.uniform(jax.random.fold_in(own, dim), (shards_of,), jnp.float32, least / len(cuts), high / len(cuts)))
        factor_of = factor_of * jnp.repeat(draws, shape[dim] // shards_of).reshape([-1 if axis == dim else 1 for axis in range(len(shape))])
    return factor_of


def scatter_about(rng, extent, scale, limit, shards=(), held_as=jnp.bfloat16):
    entries = jax.random.normal(rng, extent, jnp.float32) * scale
    if len(shards) > 0:
        entries = level_of(rng, extent, shards, -0.22, 0.18) * entries
    return jnp.clip(entries, min=-limit, max=limit).astype(held_as)


def setup_inputs(seed: int = 0) -> dict:
    keys = jax.random.split(jax.random.key(seed), 6)
    object_field = draw_object_field(jax.random.fold_in(keys[5], 71), 0)
    eigen_probes = scatter_about(keys[1], (MODES, 2, N, N), 0.35, 2.1, ((0, 2),), jnp.float32)
    coeffs = scatter_about(keys[2], (PATTERNS, 2, MODES), 1.0, 4.0, ((0, 32),), jnp.float32)
    intensities = jnp.clip(jnp.exp(math.log(1.0) - 2.9957323 * jax.random.uniform(keys[3], (PATTERNS, N, N), jnp.float32) ** level_of(keys[3], (PATTERNS, N, N), ((0, 32),), -0.2, 0.2)), 0.05, 1.0)
    positions = draw_positions(jax.random.fold_in(keys[5], 71), 0)
    return dict(object_field=object_field, eigen_probes=eigen_probes, coeffs=coeffs, intensities=intensities, positions=positions)


MAGNITUDE_FLOOR = 0.5
OBJECT_REGULARIZER = 1.0
EPSILON = 1e-05
HIGHEST_PRECISION = lax.Precision.HIGHEST

def reference(object_field, eigen_probes, coeffs, intensities, positions):
    length = eigen_probes.shape[2]
    probe_real = eigen_probes[:, 0]
    probe_imag = eigen_probes[:, 1]
    norms = lax.optimization_barrier(jnp.sum(probe_real * probe_real + probe_imag * probe_imag, axis=(1, 2)))
    anchor = jnp.zeros((), jnp.int32)
    start_terms = jnp.zeros((3,) + object_field.shape[1:], object_field.dtype)
    start_grads = jnp.zeros(eigen_probes.shape, eigen_probes.dtype)
    start_weights = jnp.zeros(norms.shape, norms.dtype)

    def visit(carry, item):
        object_terms, probe_terms, weights = carry
        coef, inten, place = item
        top = place[0].astype(jnp.int32)
        left = place[1].astype(jnp.int32)
        window = lax.dynamic_slice(object_field, (anchor, top, left), (2, length, length))
        coef_real = coef[0]
        coef_imag = coef[1]
        real_part = jnp.tensordot(coef_real, probe_real, axes=1, precision=HIGHEST_PRECISION) - jnp.tensordot(coef_imag, probe_imag, axes=1, precision=HIGHEST_PRECISION)
        imag_part = jnp.tensordot(coef_real, probe_imag, axes=1, precision=HIGHEST_PRECISION) + jnp.tensordot(coef_imag, probe_real, axes=1, precision=HIGHEST_PRECISION)
        obj_real = window[0]
        obj_imag = window[1]
        wave_real = real_part * obj_real - imag_part * obj_imag
        wave_imag = real_part * obj_imag + imag_part * obj_real
        far = jnp.fft.fft2(lax.complex(wave_real, wave_imag), norm='ortho')
        magnitude = jnp.abs(far)
        fixed = far * (jnp.sqrt(inten) / jnp.maximum(magnitude, MAGNITUDE_FLOOR))
        back = jnp.fft.ifft2(fixed, norm='ortho')
        delta_real = jnp.real(back) - wave_real
        delta_imag = jnp.imag(back) - wave_imag
        numer_real = real_part * delta_real + imag_part * delta_imag
        numer_imag = real_part * delta_imag - imag_part * delta_real
        lit = real_part * real_part + imag_part * imag_part
        piece = jnp.stack([numer_real, numer_imag, lit])
        current = lax.dynamic_slice(object_terms, (anchor, top, left), (3, length, length))
        object_terms = lax.dynamic_update_slice(object_terms, current + piece, (anchor, top, left))
        grad_real = obj_real * delta_real + obj_imag * delta_imag
        grad_imag = obj_real * delta_imag - obj_imag * delta_real
        weight = jnp.mean(obj_real * obj_real + obj_imag * obj_imag)
        term_real = coef_real[:, None, None] * grad_real + coef_imag[:, None, None] * grad_imag
        term_imag = coef_real[:, None, None] * grad_imag - coef_imag[:, None, None] * grad_real
        probe_terms = probe_terms + jnp.stack([term_real, term_imag], axis=1)
        weights = weights + (coef_real * coef_real + coef_imag * coef_imag) * weight
        inner_real = lax.optimization_barrier(jnp.sum(probe_real * grad_real + probe_imag * grad_imag, axis=(1, 2)))
        inner_imag = lax.optimization_barrier(jnp.sum(probe_real * grad_imag - probe_imag * grad_real, axis=(1, 2)))
        denominator = norms * weight + EPSILON
        updated = jnp.stack([coef_real + inner_real / denominator, coef_imag + inner_imag / denominator])
        return ((object_terms, probe_terms, weights), updated)
    carry, coeffs_new = lax.scan(visit, (start_terms, start_grads, start_weights), (coeffs, intensities, positions))
    object_terms, probe_terms, weights = carry
    object_new = object_field + object_terms[:2] / (object_terms[2] + OBJECT_REGULARIZER)
    probes_new = eigen_probes + probe_terms / weights[:, None, None, None]
    return (object_new, probes_new, coeffs_new)
```

```python
import functools
import math

import jax
import jax.numpy as jnp
import ml_dtypes
import numpy as np
from jax import lax
from jax.experimental import pallas as pl
from jax.experimental.pallas import tpu as pltpu
from jax.sharding import PartitionSpec as P

MAGNITUDE_FLOOR = 0.5
OBJECT_REGULARIZER = 1.0
EPSILON = 1e-05
MESH = pl.DeviceIdType.MESH
BLOCK = 32
EXTRA = 8
VMEM_BYTES = 56 * 1024 * 1024


def dft_tables(length):
    indices = np.arange(length)
    angle = (indices[:, None] * indices[None, :] % length) * (2.0 * math.pi / length)
    cosine = np.cos(angle) / math.sqrt(length)
    sine = -np.sin(angle) / math.sqrt(length)
    right = np.block([[cosine, sine], [-sine, cosine]])
    left = np.block([[cosine, -sine], [sine, cosine]])
    found = []
    for table in (right, left):
        high = table.astype(ml_dtypes.bfloat16)
        low = (table - high.astype(np.float64)).astype(ml_dtypes.bfloat16)
        found += [high, low]
    return found


def radices(count):
    rest = count // 2
    first = 1
    while first * first * 4 <= rest:
        first *= 2
    return first, rest // first


def gather_kernel(scans, modes, probe_ref, object_ref, gathered_ref, next_ref, *sems):
    send_y, recv_y, send_c, recv_c, send_o, recv_o = sems
    s = lax.axis_index("scan")
    m = lax.axis_index("mode")
    half = probe_ref.shape[0] // 2
    core = lax.rem(s, 2)
    sibling = s + 1 - 2 * core
    rows = pl.ds(pl.multiple_of(core * half, half), half)
    barrier = pltpu.get_barrier_semaphore()
    pl.semaphore_signal(barrier, inc=1, device_id=(sibling, m), device_id_type=MESH)
    for step in range(1, modes):
        other = lax.rem(m + step, modes)
        pl.semaphore_signal(barrier, inc=1, device_id=(s, other), device_id_type=MESH)

    @pl.when(s > 0)
    def _():
        pl.semaphore_signal(barrier, inc=1, device_id=(s - 1, m), device_id_type=MESH)

    @pl.when(s < scans - 1)
    def _():
        pl.semaphore_signal(barrier, inc=1, device_id=(s + 1, m), device_id_type=MESH)

    inner = jnp.minimum(s, 1) + jnp.minimum(scans - 1 - s, 1)
    pl.semaphore_wait(barrier, modes + inner)

    def object_copy(target):
        return pltpu.make_async_remote_copy(
            src_ref=object_ref, dst_ref=next_ref, send_sem=send_o, recv_sem=recv_o,
            device_id=(target, m), device_id_type=MESH)

    def mode_copy(step):
        return pltpu.make_async_remote_copy(
            src_ref=probe_ref.at[rows], dst_ref=gathered_ref.at[m, rows],
            send_sem=send_y.at[step - 1], recv_sem=recv_y.at[step - 1],
            device_id=(s, lax.rem(m + step, modes)), device_id_type=MESH)

    def sibling_copy(step):
        source = lax.rem(m + modes - step, modes)
        return pltpu.make_async_remote_copy(
            src_ref=gathered_ref.at[source, rows], dst_ref=gathered_ref.at[source, rows],
            send_sem=send_c.at[step - 1], recv_sem=recv_c.at[step - 1],
            device_id=(sibling, m), device_id_type=MESH)

    for step in range(1, modes):
        mode_copy(step).start()

    @pl.when(s > 0)
    def _():
        object_copy(s - 1).start()

    gathered_ref[m] = probe_ref[...]
    for step in range(1, modes):
        mode_copy(step).wait_recv()
        sibling_copy(step).start()
    for step in range(1, modes):
        mode_copy(step).wait_send()
        sibling_copy(step).wait_send()
        sibling_copy(step).wait_recv()

    @pl.when(s > 0)
    def _():
        object_copy(s - 1).wait_send()

    @pl.when(s < scans - 1)
    def _():
        object_copy(s + 1).wait_recv()


def compute_kernel(modes, place_ref, coef_ref, probe_ref, own_ref, next_ref, inten_ref,
                   rh_ref, rl_ref, lh_ref, ll_ref, terms_ref, grad_ref, coef_out_ref,
                   ext_ref, wave_ref, window_ref, mixed_ref, flat_ref, tall_ref, out_ref,
                   inner_ref, weight_ref, norm_ref):
    count, length = inten_ref.shape[0], inten_ref.shape[1]
    columns = own_ref.shape[2]
    blocks = length // BLOCK
    ext_ref[:, :length] = own_ref[...]
    ext_ref[:, length:] = next_ref[...]
    terms_ref[...] = jnp.zeros_like(terms_ref)
    grad_ref[...] = jnp.zeros_like(grad_ref)

    def folded(value):
        return jnp.sum(value.reshape(BLOCK // 8, 8, length), axis=0)

    def split(value):
        high = value.astype(jnp.bfloat16)
        return high, (value - high.astype(jnp.float32)).astype(jnp.bfloat16)

    def put_flat(rows, real, imag):
        for slot, value in enumerate((real, imag)):
            high, low = split(value)
            flat_ref[rows, slot * length:(slot + 1) * length] = high
            flat_ref[rows, (2 + slot) * length:(3 + slot) * length] = low

    def dot(a, b):
        return jnp.dot(a, b, preferred_element_type=jnp.float32)

    def right_apply(high_ref, low_ref):
        high = flat_ref[:, :2 * length]
        low = flat_ref[:, 2 * length:]
        result = dot(high, high_ref[...]) + dot(low, high_ref[...]) + dot(high, low_ref[...])
        for slot in range(2):
            part_high, part_low = split(result[:, slot * length:(slot + 1) * length])
            tall_ref[slot * length:(slot + 1) * length] = part_high
            tall_ref[(2 + slot) * length:(3 + slot) * length] = part_low

    def left_apply(high_ref, low_ref):
        high = tall_ref[:2 * length]
        low = tall_ref[2 * length:]
        out_ref[...] = dot(high_ref[...], high) + dot(high_ref[...], low) + dot(low_ref[...], high)

    norm_ref[...] = jnp.zeros_like(norm_ref)

    def norms(index, carry):
        for mode in range(modes):
            rows = pl.ds(pl.multiple_of(index * BLOCK, BLOCK), BLOCK)
            value = probe_ref[mode, rows]
            norm_ref[mode] += folded(value * value)
        return carry

    lax.fori_loop(0, 2 * blocks, norms, 0)

    def pattern(b, carry):
        top = place_ref[b, 0]
        left = place_ref[b, 1]
        back_shift = lax.rem(columns - left, columns)
        within = lax.rem(top, 8)
        top_tile = top - within
        up_shift = lax.rem(8 - within, 8)
        sublane = lax.broadcasted_iota(jnp.int32, (BLOCK // 8, 8, length), 1)
        wide = lax.broadcasted_iota(jnp.int32, (BLOCK // 8 + 1, 8, columns), 1)
        inner_ref[...] = jnp.zeros_like(inner_ref)
        weight_ref[...] = jnp.zeros_like(weight_ref)

        def first(index, carry):
            base = pl.multiple_of(index * BLOCK, BLOCK)
            rows = pl.ds(base, BLOCK)
            lower = pl.ds(pl.multiple_of(base + length, BLOCK), BLOCK)
            pr = jnp.zeros((BLOCK, length), jnp.float32)
            pi = jnp.zeros((BLOCK, length), jnp.float32)
            for mode in range(modes):
                cr, ci = coef_ref[b, 0, mode], coef_ref[b, 1, mode]
                ur, ui = probe_ref[mode, rows], probe_ref[mode, lower]
                pr = pr + cr * ur - ci * ui
                pi = pi + cr * ui + ci * ur
            window = []
            for part in range(2):
                strip = ext_ref[part, pl.ds(pl.multiple_of(top_tile + base, 8), BLOCK + 8), :]
                strip = pltpu.roll(strip, back_shift, 1)[:, :length]
                turned = pltpu.roll(strip.reshape(BLOCK // 8 + 1, 8, length), up_shift, 1)
                kept = jnp.where(sublane < 8 - within, turned[:-1], turned[1:])
                window.append(kept.reshape(BLOCK, length))
            wr, wi = window
            window_ref[rows], window_ref[lower] = wr, wi
            mixed_ref[rows], mixed_ref[lower] = pr, pi
            weight_ref[...] += folded(wr * wr + wi * wi)
            real = pr * wr - pi * wi
            imag = pr * wi + pi * wr
            wave_ref[rows], wave_ref[lower] = real, imag
            put_flat(rows, real, imag)
            return carry

        lax.fori_loop(0, blocks, first, 0)
        right_apply(rh_ref, rl_ref)
        left_apply(lh_ref, ll_ref)

        def second(index, carry):
            base = pl.multiple_of(index * BLOCK, BLOCK)
            rows = pl.ds(base, BLOCK)
            lower = pl.ds(pl.multiple_of(base + length, BLOCK), BLOCK)
            real, imag = out_ref[rows], out_ref[lower]
            power = jnp.maximum(real * real + imag * imag, MAGNITUDE_FLOOR * MAGNITUDE_FLOOR)
            factor = jnp.sqrt(inten_ref[b, rows] / power)
            put_flat(rows, real * factor, imag * factor)
            return carry

        lax.fori_loop(0, blocks, second, 0)
        right_apply(lh_ref, ll_ref)
        left_apply(rh_ref, rl_ref)

        def third(index, carry):
            base = pl.multiple_of(index * BLOCK, BLOCK)
            rows = pl.ds(base, BLOCK)
            lower = pl.ds(pl.multiple_of(base + length, BLOCK), BLOCK)
            dr = out_ref[rows] - wave_ref[rows]
            di = out_ref[lower] - wave_ref[lower]
            pr, pi = mixed_ref[rows], mixed_ref[lower]
            wr, wi = window_ref[rows], window_ref[lower]
            pieces = (pr * dr + pi * di, pr * di - pi * dr, pr * pr + pi * pi)
            for part, piece in enumerate(pieces):
                padded = jnp.concatenate(
                    [piece, jnp.zeros((BLOCK, columns - length), jnp.float32)], axis=1)
                padded = pltpu.roll(padded, left, 1).reshape(BLOCK // 8, 8, columns)
                padded = pltpu.roll(padded, within, 1)
                edge = jnp.zeros((1, 8, columns), jnp.float32)
                placed = jnp.where(
                    wide >= within,
                    jnp.concatenate([padded, edge], axis=0),
                    jnp.concatenate([edge, padded], axis=0))
                spot = pl.ds(pl.multiple_of(top_tile + base, 8), BLOCK + 8)
                terms_ref[part, spot, :] += placed.reshape(BLOCK + 8, columns)
            gr = wr * dr + wi * di
            gi = wr * di - wi * dr
            for mode in range(modes):
                cr, ci = coef_ref[b, 0, mode], coef_ref[b, 1, mode]
                ur, ui = probe_ref[mode, rows], probe_ref[mode, lower]
                grad_ref[0, mode, rows] += cr * gr + ci * gi
                grad_ref[1, mode, rows] += cr * gi - ci * gr
                inner_ref[mode, 0] += folded(ur * gr + ui * gi)
                inner_ref[mode, 1] += folded(ur * gi - ui * gr)
            return carry

        lax.fori_loop(0, blocks, third, 0)

        def total(value):
            return jnp.sum(jnp.sum(value, axis=1, keepdims=True), axis=0, keepdims=True)

        weight = total(weight_ref[...]) * (1.0 / (length * length))
        lanes = lax.broadcasted_iota(jnp.int32, (1, modes), 1)
        found = [jnp.zeros((1, modes), jnp.float32)] * 2
        for mode in range(modes):
            cr, ci = coef_ref[b, 0, mode], coef_ref[b, 1, mode]
            denominator = total(norm_ref[mode]) * weight + EPSILON
            for part, c in enumerate((cr, ci)):
                value = c + total(inner_ref[mode, part]) / denominator
                found[part] = jnp.where(lanes == mode, value, found[part])
            share = jnp.broadcast_to((cr * cr + ci * ci) * weight, (1, length))
            for part in range(2):
                grad_ref[part, mode, length:] += jnp.broadcast_to(share, (EXTRA, length))
        coef_out_ref[b] = jnp.concatenate(found, axis=0)
        return carry

    lax.fori_loop(0, count, pattern, 0)


def reduce_kernel(scans, modes, terms_ref, grad_ref, object_ref, probe_ref,
                  object_out_ref, probe_out_ref,
                  core_in, mode_in, stage1, in1, stage2, in2, shift_in, stage_n, numer_in,
                  send_g, recv_g, send_1, recv_1, send_2, recv_2, send_b, recv_b,
                  send_s, recv_s, send_n, recv_n, send_a, recv_a):
    s = lax.axis_index("scan")
    m = lax.axis_index("mode")
    r1, r2 = radices(scans)
    length = object_ref.shape[1]
    d0 = lax.rem(s, 2)
    d1 = lax.rem(s // 2, r1)
    d2 = s // (2 * r1)
    b1, b2 = length // r1, length // (r1 * r2)
    rows_m = length // modes
    sibling = (s + 1 - 2 * d0, m)

    def peer1(step):
        return ((d2 * r1 + lax.rem(d1 + step, r1)) * 2 + d0, m)

    def peer2(step):
        return ((lax.rem(d2 + step, r2) * r1 + d1) * 2 + d0, m)

    def peer_m(step):
        return (s, lax.rem(m + step, modes))

    peers = [sibling] + [peer1(i) for i in range(1, r1)] + [peer2(i) for i in range(1, r2)]
    peers += [peer_m(i) for i in range(1, modes)]
    barrier = pltpu.get_barrier_semaphore()
    for peer in peers:
        pl.semaphore_signal(barrier, inc=1, device_id=peer, device_id_type=MESH)

    @pl.when(s > 0)
    def _():
        pl.semaphore_signal(barrier, inc=1, device_id=(s - 1, m), device_id_type=MESH)

    @pl.when(s < scans - 1)
    def _():
        pl.semaphore_signal(barrier, inc=1, device_id=(s + 1, m), device_id_type=MESH)

    inner = jnp.minimum(s, 1) + jnp.minimum(scans - 1 - s, 1)
    pl.semaphore_wait(barrier, len(peers) + inner)

    def remote(src, dst, send, recv, peer):
        return pltpu.make_async_remote_copy(
            src_ref=src, dst_ref=dst, send_sem=send, recv_sem=recv,
            device_id=peer, device_id_type=MESH)

    def chunk(owner):
        return pl.ds(pl.multiple_of(owner * rows_m, rows_m), rows_m)

    def shift_copy(step, target):
        owner = lax.rem(m + step, modes)
        away = pl.ds(pl.multiple_of(length + owner * rows_m, rows_m), rows_m)
        return remote(terms_ref.at[:, away], shift_in.at[:, chunk(owner)],
                      send_s.at[step - 1], recv_s.at[step - 1], (target, m))

    sends = []
    core_copy = remote(grad_ref.at[1 - d0], core_in, send_g.at[0], recv_g.at[0], sibling)
    core_copy.start()
    sends.append(core_copy)

    @pl.when(s < scans - 1)
    def _():
        for step in range(1, modes + 1):
            shift_copy(step, s + 1).start()

    @pl.when(s == 0)
    def _():
        shift_in[...] = jnp.zeros_like(shift_in)

    def shift_wait(step):
        @pl.when(s > 0)
        def _():
            shift_copy(step, s - 1).wait_recv()

    core_copy.wait_recv()
    mode_copies = []
    for step in range(1, modes):
        owner = lax.rem(m + step, modes)
        core_in[owner] = core_in[owner] + grad_ref[d0, owner]
        copy = remote(core_in.at[owner], mode_in.at[step - 1],
                      send_g.at[step], recv_g.at[step], peer_m(step))
        copy.start()
        mode_copies.append(copy)
    numer_copies = []
    for step in range(1, modes):
        owner = lax.rem(m + step, modes)
        shift_wait(step)
        stage_n[step - 1] = terms_ref[:, chunk(owner)] + shift_in[:, chunk(owner)]
        copy = remote(stage_n.at[step - 1], numer_in.at[step - 1],
                      send_n.at[step - 1], recv_n.at[step - 1], peer_m(step))
        copy.start()
        numer_copies.append(copy)
    total = core_in[m] + grad_ref[d0, m]
    for step in range(1, modes):
        mode_copies[step - 1].wait_recv()
        total = total + mode_in[step - 1]
    for index in range(r1):
        stage1[index, :b1] = total[index * b1:(index + 1) * b1]
        stage1[index, b1:] = total[length:]
    copies1 = []
    for step in range(1, r1):
        copy = remote(stage1.at[lax.rem(d1 + step, r1)], in1.at[step - 1],
                      send_1.at[step - 1], recv_1.at[step - 1], peer1(step))
        copy.start()
        copies1.append(copy)
    total = stage1[d1]
    for step in range(1, r1):
        copies1[step - 1].wait_recv()
        total = total + in1[step - 1]
    for index in range(r2):
        stage2[index, :b2] = total[index * b2:(index + 1) * b2]
        stage2[index, b2:] = total[b1:]
    copies2 = []
    for step in range(1, r2):
        copy = remote(stage2.at[lax.rem(d2 + step, r2)], in2.at[step - 1],
                      send_2.at[step - 1], recv_2.at[step - 1], peer2(step))
        copy.start()
        copies2.append(copy)
    total = stage2[d2]
    for step in range(1, r2):
        copies2[step - 1].wait_recv()
        total = total + in2[step - 1]
    block0 = pl.ds(pl.multiple_of(d0 * length, length), length)
    start1 = d0 * length + d1 * b1
    block1 = pl.ds(pl.multiple_of(start1, b1), b1)
    block2 = pl.ds(pl.multiple_of(start1 + d2 * b2, b2), b2)
    probe_out_ref[block2] = probe_ref[block2] + total[:b2] / total[b2:b2 + 1]
    back2 = []
    for step in range(1, r2):
        copy = remote(probe_out_ref.at[block2], probe_out_ref.at[block2],
                      send_b.at[step - 1], recv_b.at[step - 1], peer2(step))
        copy.start()
        back2.append(copy)
    shift_wait(modes)
    for step in range(1, modes):
        numer_copies[step - 1].wait_recv()
    mine = chunk(m)

    def owned(part):
        value = terms_ref[part, mine] + shift_in[part, mine]
        for step in range(1, modes):
            value = value + numer_in[step - 1, part]
        return value

    scale = owned(2) + OBJECT_REGULARIZER
    for part in range(2):
        object_out_ref[part, mine] = object_ref[part, mine] + owned(part) / scale
    object_copies = []
    for step in range(1, modes):
        copy = remote(object_out_ref.at[:, mine], object_out_ref.at[:, mine],
                      send_a.at[step - 1], recv_a.at[step - 1], peer_m(step))
        copy.start()
        object_copies.append(copy)
    for copy in back2:
        copy.wait_recv()
    back1 = []
    for step in range(1, r1):
        slot = r2 - 1 + step - 1
        copy = remote(probe_out_ref.at[block1], probe_out_ref.at[block1],
                      send_b.at[slot], recv_b.at[slot], peer1(step))
        copy.start()
        back1.append(copy)
    for copy in back1:
        copy.wait_recv()
    slot = r2 + r1 - 2
    back0 = remote(probe_out_ref.at[block0], probe_out_ref.at[block0],
                   send_b.at[slot], recv_b.at[slot], sibling)
    back0.start()
    back0.wait_recv()
    for copy in object_copies:
        copy.wait_recv()

    @pl.when(s < scans - 1)
    def _():
        for step in range(1, modes + 1):
            shift_copy(step, s + 1).wait_send()

    for copy in sends + mode_copies + numer_copies + copies1 + copies2 + back2 + back1:
        copy.wait_send()
    for copy in object_copies + [back0]:
        copy.wait_send()


def on_device(scans, modes, object_field, eigen_probes, coeffs, intensities, positions):
    length = eigen_probes.shape[2]
    columns = object_field.shape[2]
    f32 = jnp.float32
    vmem = pl.BlockSpec(memory_space=pltpu.VMEM)
    smem = pl.BlockSpec(memory_space=pltpu.SMEM)
    dma = pltpu.SemaphoreType.DMA
    probe = eigen_probes.reshape(2 * length, length)
    others = max(modes - 1, 1)
    r1, r2 = radices(scans)
    b1, b2 = length // r1, length // (r1 * r2)
    gathered, following = pl.pallas_call(
        functools.partial(gather_kernel, scans, modes),
        out_shape=(
            jax.ShapeDtypeStruct((modes, 2 * length, length), f32),
            jax.ShapeDtypeStruct(object_field.shape, f32),
        ),
        in_specs=[vmem] * 2,
        out_specs=(vmem, vmem),
        scratch_shapes=[dma((others,))] * 4 + [dma, dma],
        compiler_params=pltpu.CompilerParams(
            collective_id=0, has_side_effects=True, vmem_limit_bytes=VMEM_BYTES),
        name="gather_probes",
    )(probe, object_field)
    row_start = positions[:, 0] - lax.axis_index("scan") * length
    place = jnp.stack([row_start, positions[:, 1]], axis=1)
    tables = [jnp.asarray(table) for table in dft_tables(length)]
    terms, grads, coeffs_new = pl.pallas_call(
        functools.partial(compute_kernel, modes),
        out_shape=(
            jax.ShapeDtypeStruct((3, 2 * length, columns), f32),
            jax.ShapeDtypeStruct((2, modes, length + EXTRA, length), f32),
            jax.ShapeDtypeStruct(coeffs.shape, f32),
        ),
        in_specs=[smem, smem] + [vmem] * 8,
        out_specs=(vmem, vmem, vmem),
        scratch_shapes=[
            pltpu.VMEM((2, 2 * length, columns), f32),
            pltpu.VMEM((2 * length, length), f32),
            pltpu.VMEM((2 * length, length), f32),
            pltpu.VMEM((2 * length, length), f32),
            pltpu.VMEM((length, 4 * length), jnp.bfloat16),
            pltpu.VMEM((4 * length, length), jnp.bfloat16),
            pltpu.VMEM((2 * length, length), f32),
            pltpu.VMEM((modes, 2, 8, length), f32),
            pltpu.VMEM((8, length), f32),
            pltpu.VMEM((modes, 8, length), f32),
        ],
        compiler_params=pltpu.CompilerParams(vmem_limit_bytes=VMEM_BYTES),
        name="local_terms",
    )(place, coeffs, gathered, object_field, following, intensities, *tables)
    rows_m = length // modes
    object_new, probes_new = pl.pallas_call(
        functools.partial(reduce_kernel, scans, modes),
        out_shape=(
            jax.ShapeDtypeStruct(object_field.shape, f32),
            jax.ShapeDtypeStruct((2 * length, length), f32),
        ),
        in_specs=[vmem] * 4,
        out_specs=(vmem, vmem),
        scratch_shapes=[
            pltpu.VMEM((modes, length + EXTRA, length), f32),
            pltpu.VMEM((others, length + EXTRA, length), f32),
            pltpu.VMEM((r1, b1 + EXTRA, length), f32),
            pltpu.VMEM((max(r1 - 1, 1), b1 + EXTRA, length), f32),
            pltpu.VMEM((r2, b2 + EXTRA, length), f32),
            pltpu.VMEM((max(r2 - 1, 1), b2 + EXTRA, length), f32),
            pltpu.VMEM((3, length, columns), f32),
            pltpu.VMEM((others, 3, rows_m, columns), f32),
            pltpu.VMEM((others, 3, rows_m, columns), f32),
            dma((modes,)), dma((modes,)),
            dma((max(r1 - 1, 1),)), dma((max(r1 - 1, 1),)),
            dma((max(r2 - 1, 1),)), dma((max(r2 - 1, 1),)),
            dma((r1 + r2 - 1,)), dma((r1 + r2 - 1,)),
            dma((modes,)), dma((modes,)),
            dma((others,)), dma((others,)),
            dma((others,)), dma((others,)),
        ],
        compiler_params=pltpu.CompilerParams(
            collective_id=1, has_side_effects=True, vmem_limit_bytes=VMEM_BYTES),
        name="reduce_terms",
    )(terms, grads, object_field, probe)
    return object_new, probes_new.reshape(eigen_probes.shape), coeffs_new


def solution(mesh):
    return jax.shard_map(
        functools.partial(on_device, mesh.shape["scan"], mesh.shape["mode"]),
        mesh=mesh,
        in_specs=(
            P(None, "scan", None),
            P("mode", None, None, None),
            P(("scan", "mode"), None, None),
            P(("scan", "mode"), None, None),
            P(("scan", "mode"), None),
        ),
        out_specs=(
            P(None, "scan", None),
            P("mode", None, None, None),
            P(("scan", "mode"), None, None),
        ),
        check_vma=False,
    )
```

```python
import functools
import math

import jax
import jax.numpy as jnp
import ml_dtypes
import numpy as np
from jax import lax
from jax.experimental import pallas as pl
from jax.experimental.pallas import tpu as pltpu
from jax.sharding import PartitionSpec as P

MAGNITUDE_FLOOR = 0.5
OBJECT_REGULARIZER = 1.0
EPSILON = 1e-05
MESH = pl.DeviceIdType.MESH
BLOCK = 32
EXTRA = 8
VMEM_BYTES = 56 * 1024 * 1024


def dft_tables(length):
    indices = np.arange(length)
    angle = (indices[:, None] * indices[None, :] % length) * (2.0 * math.pi / length)
    cosine = np.cos(angle) / math.sqrt(length)
    sine = -np.sin(angle) / math.sqrt(length)
    right = np.block([[cosine, sine], [-sine, cosine]])
    left = np.block([[cosine, -sine], [sine, cosine]])
    found = []
    for table in (right, left):
        high = table.astype(ml_dtypes.bfloat16)
        low = (table - high.astype(np.float64)).astype(ml_dtypes.bfloat16)
        found += [high, low]
    return found


def radices(count):
    rest = count // 2
    first = 1
    while first * first * 4 <= rest:
        first *= 2
    return first, rest // first


def gather_kernel(scans, modes, probe_ref, object_ref, inten_ref, place_ref, coef_ref,
                  gathered_ref, next_ref, inten_out_ref, place_out_ref, coef_out_ref,
                  send_y, recv_y, send_c, recv_c, send_o, recv_o, send_t, recv_t):
    count = inten_ref.shape[0]
    s = lax.axis_index("scan")
    m = lax.axis_index("mode")
    half = probe_ref.shape[0] // 2
    core = lax.rem(s, 2)
    sibling = s + 1 - 2 * core
    rows = pl.ds(pl.multiple_of(core * half, half), half)
    barrier = pltpu.get_barrier_semaphore()
    pl.semaphore_signal(barrier, inc=1, device_id=(sibling, m), device_id_type=MESH)
    for step in range(1, modes):
        other = lax.rem(m + step, modes)
        pl.semaphore_signal(barrier, inc=1, device_id=(s, other), device_id_type=MESH)

    @pl.when(s > 0)
    def _():
        pl.semaphore_signal(barrier, inc=1, device_id=(s - 1, m), device_id_type=MESH)

    @pl.when(s < scans - 1)
    def _():
        pl.semaphore_signal(barrier, inc=1, device_id=(s + 1, m), device_id_type=MESH)

    inner = jnp.minimum(s, 1) + jnp.minimum(scans - 1 - s, 1)
    pl.semaphore_wait(barrier, modes + inner)

    def object_copy(target):
        return pltpu.make_async_remote_copy(
            src_ref=object_ref, dst_ref=next_ref, send_sem=send_o, recv_sem=recv_o,
            device_id=(target, m), device_id_type=MESH)

    def mode_copy(step):
        return pltpu.make_async_remote_copy(
            src_ref=probe_ref.at[rows], dst_ref=gathered_ref.at[m, rows],
            send_sem=send_y.at[step - 1], recv_sem=recv_y.at[step - 1],
            device_id=(s, lax.rem(m + step, modes)), device_id_type=MESH)

    def sibling_copy(step):
        source = lax.rem(m + modes - step, modes)
        return pltpu.make_async_remote_copy(
            src_ref=gathered_ref.at[source, rows], dst_ref=gathered_ref.at[source, rows],
            send_sem=send_c.at[step - 1], recv_sem=recv_c.at[step - 1],
            device_id=(sibling, m), device_id_type=MESH)

    held = pl.ds(m * count, count)
    tile_pairs = ((place_ref, place_out_ref.at[m]), (coef_ref, coef_out_ref.at[m]),
                  (inten_ref, inten_out_ref.at[held]))

    def tile_copies(step):
        return [pltpu.make_async_remote_copy(
            src_ref=src, dst_ref=dst,
            send_sem=send_t.at[step - 1, slot], recv_sem=recv_t.at[step - 1, slot],
            device_id=(s, lax.rem(m + step, modes)), device_id_type=MESH)
            for slot, (src, dst) in enumerate(tile_pairs)]

    for step in range(1, modes):
        mode_copy(step).start()

    @pl.when(s > 0)
    def _():
        object_copy(s - 1).start()

    for step in range(1, modes):
        for copy in tile_copies(step):
            copy.start()

    gathered_ref[m] = probe_ref[...]
    place_out_ref[m] = place_ref[...]
    coef_out_ref[m] = coef_ref[...]
    inten_out_ref[held] = inten_ref[...]
    for step in range(1, modes):
        mode_copy(step).wait_recv()
        sibling_copy(step).start()
    for step in range(1, modes):
        mode_copy(step).wait_send()
        sibling_copy(step).wait_send()
        sibling_copy(step).wait_recv()
        for copy in tile_copies(step):
            copy.wait()

    @pl.when(s > 0)
    def _():
        object_copy(s - 1).wait_send()

    @pl.when(s < scans - 1)
    def _():
        object_copy(s + 1).wait_recv()


def compute_kernel(modes, place_ref, coef_ref, probe_ref, own_ref, next_ref, inten_ref,
                   rh_ref, rl_ref, lh_ref, ll_ref, terms_ref, grad_ref, coef_out_ref,
                   ext_ref, wave_ref, window_ref, mixed_ref, flat_ref, tall_ref, out_ref,
                   inner_ref, weight_ref, norm_ref):
    patterns, length = inten_ref.shape[0], inten_ref.shape[1]
    count = patterns // modes
    me = lax.axis_index("mode")
    tile_top = lax.axis_index("scan") * length
    columns = own_ref.shape[2]
    blocks = length // BLOCK
    ext_ref[:, :length] = own_ref[...]
    ext_ref[:, length:] = next_ref[...]
    terms_ref[...] = jnp.zeros_like(terms_ref)
    grad_ref[...] = jnp.zeros_like(grad_ref)

    def folded(value):
        return jnp.sum(value.reshape(BLOCK // 8, 8, length), axis=0)

    def split(value):
        high = value.astype(jnp.bfloat16)
        return high, (value - high.astype(jnp.float32)).astype(jnp.bfloat16)

    def put_flat(rows, real, imag):
        for slot, value in enumerate((real, imag)):
            high, low = split(value)
            flat_ref[rows, slot * length:(slot + 1) * length] = high
            flat_ref[rows, (2 + slot) * length:(3 + slot) * length] = low

    def dot(a, b):
        return jnp.dot(a, b, preferred_element_type=jnp.float32)

    def right_apply(high_ref, low_ref):
        field = flat_ref[...]
        table = high_ref[...]
        result = dot(jnp.concatenate([field, field[:, :2 * length]], axis=1),
                     jnp.concatenate([table, table, low_ref[...]], axis=0))
        for slot in range(2):
            part_high, part_low = split(result[:, slot * length:(slot + 1) * length])
            tall_ref[slot * length:(slot + 1) * length] = part_high
            tall_ref[(2 + slot) * length:(3 + slot) * length] = part_low

    def left_apply(high_ref, low_ref):
        field = tall_ref[...]
        table = high_ref[...]
        out_ref[...] = dot(jnp.concatenate([table, table, low_ref[...]], axis=1),
                           jnp.concatenate([field, field[:2 * length]], axis=0))

    norm_ref[...] = jnp.zeros_like(norm_ref)

    def norms(index, carry):
        for mode in range(modes):
            rows = pl.ds(pl.multiple_of(index * BLOCK, BLOCK), BLOCK)
            value = probe_ref[mode, rows]
            norm_ref[mode] += folded(value * value)
        return carry

    lax.fori_loop(0, 2 * blocks, norms, 0)

    def pattern(own, index, carry):
        b = lax.rem(index, count)
        owner = lax.rem(me + index // count, modes)
        b_all = owner * count + b

        def coef(mode):
            return coef_ref[owner, b, mode], coef_ref[owner, b, modes + mode]

        top = place_ref[owner, b, 0] - tile_top
        left = place_ref[owner, b, 1]
        back_shift = lax.rem(columns - left, columns)
        within = lax.rem(top, 8)
        top_tile = top - within
        up_shift = lax.rem(8 - within, 8)
        sublane = lax.broadcasted_iota(jnp.int32, (BLOCK // 8, 8, length), 1)
        wide = lax.broadcasted_iota(jnp.int32, (BLOCK // 8 + 1, 8, columns), 1)
        inner_ref[...] = jnp.zeros_like(inner_ref)
        weight_ref[...] = jnp.zeros_like(weight_ref)

        def first(index, carry):
            base = pl.multiple_of(index * BLOCK, BLOCK)
            rows = pl.ds(base, BLOCK)
            lower = pl.ds(pl.multiple_of(base + length, BLOCK), BLOCK)
            pr = jnp.zeros((BLOCK, length), jnp.float32)
            pi = jnp.zeros((BLOCK, length), jnp.float32)
            for mode in range(modes):
                cr, ci = coef(mode)
                ur, ui = probe_ref[mode, rows], probe_ref[mode, lower]
                pr = pr + cr * ur - ci * ui
                pi = pi + cr * ui + ci * ur
            window = []
            for part in range(2):
                strip = ext_ref[part, pl.ds(pl.multiple_of(top_tile + base, 8), BLOCK + 8), :]
                strip = pltpu.roll(strip, back_shift, 1)[:, :length]
                turned = pltpu.roll(strip.reshape(BLOCK // 8 + 1, 8, length), up_shift, 1)
                kept = jnp.where(sublane < 8 - within, turned[:-1], turned[1:])
                window.append(kept.reshape(BLOCK, length))
            wr, wi = window
            window_ref[rows], window_ref[lower] = wr, wi
            mixed_ref[rows], mixed_ref[lower] = pr, pi
            weight_ref[...] += folded(wr * wr + wi * wi)
            real = pr * wr - pi * wi
            imag = pr * wi + pi * wr
            wave_ref[rows], wave_ref[lower] = real, imag
            put_flat(rows, real, imag)
            return carry

        lax.fori_loop(0, blocks, first, 0)
        right_apply(rh_ref, rl_ref)
        left_apply(lh_ref, ll_ref)

        def second(index, carry):
            base = pl.multiple_of(index * BLOCK, BLOCK)
            rows = pl.ds(base, BLOCK)
            lower = pl.ds(pl.multiple_of(base + length, BLOCK), BLOCK)
            real, imag = out_ref[rows], out_ref[lower]
            power = jnp.maximum(real * real + imag * imag, MAGNITUDE_FLOOR * MAGNITUDE_FLOOR)
            factor = jnp.sqrt(inten_ref[b_all, rows] / power)
            put_flat(rows, real * factor, imag * factor)
            return carry

        lax.fori_loop(0, blocks, second, 0)
        right_apply(lh_ref, ll_ref)
        left_apply(rh_ref, rl_ref)

        def third(index, carry):
            base = pl.multiple_of(index * BLOCK, BLOCK)
            rows = pl.ds(base, BLOCK)
            lower = pl.ds(pl.multiple_of(base + length, BLOCK), BLOCK)
            dr = out_ref[rows] - wave_ref[rows]
            di = out_ref[lower] - wave_ref[lower]
            pr, pi = mixed_ref[rows], mixed_ref[lower]
            wr, wi = window_ref[rows], window_ref[lower]
            pieces = (pr * dr + pi * di, pr * di - pi * dr, pr * pr + pi * pi)
            for part, piece in enumerate(pieces):
                padded = jnp.concatenate(
                    [piece, jnp.zeros((BLOCK, columns - length), jnp.float32)], axis=1)
                padded = pltpu.roll(padded, left, 1).reshape(BLOCK // 8, 8, columns)
                padded = pltpu.roll(padded, within, 1)
                edge = jnp.zeros((1, 8, columns), jnp.float32)
                placed = jnp.where(
                    wide >= within,
                    jnp.concatenate([padded, edge], axis=0),
                    jnp.concatenate([edge, padded], axis=0))
                spot = pl.ds(pl.multiple_of(top_tile + base, 8), BLOCK + 8)
                terms_ref[part, spot, :] += placed.reshape(BLOCK + 8, columns)
            gr = wr * dr + wi * di
            gi = wr * di - wi * dr
            cr, ci = coef(me)
            grad_ref[0, rows] += cr * gr + ci * gi
            grad_ref[1, rows] += cr * gi - ci * gr
            for mode in range(modes if own else 0):
                ur, ui = probe_ref[mode, rows], probe_ref[mode, lower]
                inner_ref[mode, 0] += folded(ur * gr + ui * gi)
                inner_ref[mode, 1] += folded(ur * gi - ui * gr)
            return carry

        lax.fori_loop(0, blocks, third, 0)

        def total(value):
            return jnp.sum(jnp.sum(value, axis=1, keepdims=True), axis=0, keepdims=True)

        weight = total(weight_ref[...]) * (1.0 / (length * length))
        cr, ci = coef(me)
        share = jnp.broadcast_to((cr * cr + ci * ci) * weight, (1, length))
        for part in range(2):
            grad_ref[part, length:] += jnp.broadcast_to(share, (EXTRA, length))
        if not own:
            return carry
        lanes = lax.broadcasted_iota(jnp.int32, (1, modes), 1)
        found = [jnp.zeros((1, modes), jnp.float32)] * 2
        for mode in range(modes):
            cr, ci = coef(mode)
            denominator = total(norm_ref[mode]) * weight + EPSILON
            for part, c in enumerate((cr, ci)):
                value = c + total(inner_ref[mode, part]) / denominator
                found[part] = jnp.where(lanes == mode, value, found[part])
        coef_out_ref[b] = jnp.concatenate(found, axis=0)
        return carry

    lax.fori_loop(0, count, functools.partial(pattern, True), 0)
    lax.fori_loop(count, patterns, functools.partial(pattern, False), 0)


def reduce_kernel(scans, terms_ref, grad_ref, object_ref, probe_ref,
                  object_out_ref, probe_out_ref,
                  core_in, stage1, in1, stage2, in2, shift_in,
                  send_g, recv_g, send_1, recv_1, send_2, recv_2, send_b, recv_b,
                  send_s, recv_s):
    s = lax.axis_index("scan")
    m = lax.axis_index("mode")
    r1, r2 = radices(scans)
    length = object_ref.shape[1]
    d0 = lax.rem(s, 2)
    d1 = lax.rem(s // 2, r1)
    d2 = s // (2 * r1)
    b1, b2 = length // r1, length // (r1 * r2)
    sibling = (s + 1 - 2 * d0, m)

    def peer1(step):
        return ((d2 * r1 + lax.rem(d1 + step, r1)) * 2 + d0, m)

    def peer2(step):
        return ((lax.rem(d2 + step, r2) * r1 + d1) * 2 + d0, m)

    peers = [sibling] + [peer1(i) for i in range(1, r1)] + [peer2(i) for i in range(1, r2)]
    barrier = pltpu.get_barrier_semaphore()
    for peer in peers:
        pl.semaphore_signal(barrier, inc=1, device_id=peer, device_id_type=MESH)

    @pl.when(s > 0)
    def _():
        pl.semaphore_signal(barrier, inc=1, device_id=(s - 1, m), device_id_type=MESH)

    @pl.when(s < scans - 1)
    def _():
        pl.semaphore_signal(barrier, inc=1, device_id=(s + 1, m), device_id_type=MESH)

    inner = jnp.minimum(s, 1) + jnp.minimum(scans - 1 - s, 1)
    pl.semaphore_wait(barrier, len(peers) + inner)

    def remote(src, dst, send, recv, peer):
        return pltpu.make_async_remote_copy(
            src_ref=src, dst_ref=dst, send_sem=send, recv_sem=recv,
            device_id=peer, device_id_type=MESH)

    def shift_copy(target):
        return remote(terms_ref.at[:, pl.ds(length, length)], shift_in, send_s, recv_s, (target, m))

    sends = []
    core_copy = remote(grad_ref.at[1 - d0], core_in, send_g, recv_g, sibling)
    core_copy.start()
    sends.append(core_copy)

    @pl.when(s < scans - 1)
    def _():
        shift_copy(s + 1).start()

    @pl.when(s == 0)
    def _():
        shift_in[...] = jnp.zeros_like(shift_in)

    core_copy.wait_recv()
    total = core_in[...] + grad_ref[d0]
    for index in range(r1):
        stage1[index, :b1] = total[index * b1:(index + 1) * b1]
        stage1[index, b1:] = total[length:]
    copies1 = []
    for step in range(1, r1):
        copy = remote(stage1.at[lax.rem(d1 + step, r1)], in1.at[step - 1],
                      send_1.at[step - 1], recv_1.at[step - 1], peer1(step))
        copy.start()
        copies1.append(copy)
    total = stage1[d1]
    for step in range(1, r1):
        copies1[step - 1].wait_recv()
        total = total + in1[step - 1]
    for index in range(r2):
        stage2[index, :b2] = total[index * b2:(index + 1) * b2]
        stage2[index, b2:] = total[b1:]
    copies2 = []
    for step in range(1, r2):
        copy = remote(stage2.at[lax.rem(d2 + step, r2)], in2.at[step - 1],
                      send_2.at[step - 1], recv_2.at[step - 1], peer2(step))
        copy.start()
        copies2.append(copy)
    total = stage2[d2]
    for step in range(1, r2):
        copies2[step - 1].wait_recv()
        total = total + in2[step - 1]
    block0 = pl.ds(pl.multiple_of(d0 * length, length), length)
    start1 = d0 * length + d1 * b1
    block1 = pl.ds(pl.multiple_of(start1, b1), b1)
    block2 = pl.ds(pl.multiple_of(start1 + d2 * b2, b2), b2)
    probe_out_ref[block2] = probe_ref[block2] + total[:b2] / total[b2:b2 + 1]
    back2 = []
    for step in range(1, r2):
        copy = remote(probe_out_ref.at[block2], probe_out_ref.at[block2],
                      send_b.at[step - 1], recv_b.at[step - 1], peer2(step))
        copy.start()
        back2.append(copy)
    for copy in back2:
        copy.wait_recv()
    back1 = []
    for step in range(1, r1):
        slot = r2 - 1 + step - 1
        copy = remote(probe_out_ref.at[block1], probe_out_ref.at[block1],
                      send_b.at[slot], recv_b.at[slot], peer1(step))
        copy.start()
        back1.append(copy)
    for copy in back1:
        copy.wait_recv()
    slot = r2 + r1 - 2
    back0 = remote(probe_out_ref.at[block0], probe_out_ref.at[block0],
                   send_b.at[slot], recv_b.at[slot], sibling)
    back0.start()

    @pl.when(s > 0)
    def _():
        shift_copy(s - 1).wait_recv()

    def owned(part):
        return terms_ref[part, :length] + shift_in[part]

    scale = owned(2) + OBJECT_REGULARIZER
    for part in range(2):
        object_out_ref[part] = object_ref[part] + owned(part) / scale
    back0.wait_recv()

    @pl.when(s < scans - 1)
    def _():
        shift_copy(s + 1).wait_send()

    for copy in sends + copies1 + copies2 + back2 + back1:
        copy.wait_send()
    for copy in [back0]:
        copy.wait_send()


def on_device(scans, modes, object_field, eigen_probes, coeffs, intensities, positions):
    length = eigen_probes.shape[2]
    columns = object_field.shape[2]
    count = intensities.shape[0]
    f32 = jnp.float32
    vmem = pl.BlockSpec(memory_space=pltpu.VMEM)
    smem = pl.BlockSpec(memory_space=pltpu.SMEM)
    dma = pltpu.SemaphoreType.DMA
    probe = eigen_probes.reshape(2 * length, length)
    others = max(modes - 1, 1)
    r1, r2 = radices(scans)
    b1, b2 = length // r1, length // (r1 * r2)
    place = jnp.pad(positions, ((0, 8 - count), (0, 126)))
    coef = jnp.pad(coeffs.reshape(count, 2 * modes), ((0, 8 - count), (0, 128 - 2 * modes)))
    gathered, following, inten_all, place_all, coef_all = pl.pallas_call(
        functools.partial(gather_kernel, scans, modes),
        out_shape=(
            jax.ShapeDtypeStruct((modes, 2 * length, length), f32),
            jax.ShapeDtypeStruct(object_field.shape, f32),
            jax.ShapeDtypeStruct((modes * count, length, length), f32),
            jax.ShapeDtypeStruct((modes, 8, 128), jnp.int32),
            jax.ShapeDtypeStruct((modes, 8, 128), f32),
        ),
        in_specs=[vmem] * 5,
        out_specs=(vmem,) * 5,
        scratch_shapes=[dma((others,))] * 4 + [dma, dma, dma((others, 3)), dma((others, 3))],
        compiler_params=pltpu.CompilerParams(
            collective_id=0, has_side_effects=True, vmem_limit_bytes=VMEM_BYTES),
        name="gather_probes",
    )(probe, object_field, intensities, place, coef)
    tables = [jnp.asarray(table) for table in dft_tables(length)]
    terms, grads, coeffs_new = pl.pallas_call(
        functools.partial(compute_kernel, modes),
        out_shape=(
            jax.ShapeDtypeStruct((3, 2 * length, columns), f32),
            jax.ShapeDtypeStruct((2, length + EXTRA, length), f32),
            jax.ShapeDtypeStruct(coeffs.shape, f32),
        ),
        in_specs=[smem, smem] + [vmem] * 8,
        out_specs=(vmem, vmem, vmem),
        scratch_shapes=[
            pltpu.VMEM((2, 2 * length, columns), f32),
            pltpu.VMEM((2 * length, length), f32),
            pltpu.VMEM((2 * length, length), f32),
            pltpu.VMEM((2 * length, length), f32),
            pltpu.VMEM((length, 4 * length), jnp.bfloat16),
            pltpu.VMEM((4 * length, length), jnp.bfloat16),
            pltpu.VMEM((2 * length, length), f32),
            pltpu.VMEM((modes, 2, 8, length), f32),
            pltpu.VMEM((8, length), f32),
            pltpu.VMEM((modes, 8, length), f32),
        ],
        compiler_params=pltpu.CompilerParams(vmem_limit_bytes=VMEM_BYTES),
        name="local_terms",
    )(place_all, coef_all, gathered, object_field, following, inten_all, *tables)
    object_new, probes_new = pl.pallas_call(
        functools.partial(reduce_kernel, scans),
        out_shape=(
            jax.ShapeDtypeStruct(object_field.shape, f32),
            jax.ShapeDtypeStruct((2 * length, length), f32),
        ),
        in_specs=[vmem] * 4,
        out_specs=(vmem, vmem),
        scratch_shapes=[
            pltpu.VMEM((length + EXTRA, length), f32),
            pltpu.VMEM((r1, b1 + EXTRA, length), f32),
            pltpu.VMEM((max(r1 - 1, 1), b1 + EXTRA, length), f32),
            pltpu.VMEM((r2, b2 + EXTRA, length), f32),
            pltpu.VMEM((max(r2 - 1, 1), b2 + EXTRA, length), f32),
            pltpu.VMEM((3, length, columns), f32),
            dma, dma,
            dma((max(r1 - 1, 1),)), dma((max(r1 - 1, 1),)),
            dma((max(r2 - 1, 1),)), dma((max(r2 - 1, 1),)),
            dma((r1 + r2 - 1,)), dma((r1 + r2 - 1,)),
            dma, dma,
        ],
        compiler_params=pltpu.CompilerParams(
            collective_id=1, has_side_effects=True, vmem_limit_bytes=VMEM_BYTES),
        name="reduce_terms",
    )(terms, grads, object_field, probe)
    return object_new, probes_new.reshape(eigen_probes.shape), coeffs_new


def solution(mesh):
    return jax.shard_map(
        functools.partial(on_device, mesh.shape["scan"], mesh.shape["mode"]),
        mesh=mesh,
        in_specs=(
            P(None, "scan", None),
            P("mode", None, None, None),
            P(("scan", "mode"), None, None),
            P(("scan", "mode"), None, None),
            P(("scan", "mode"), None),
        ),
        out_specs=(
            P(None, "scan", None),
            P("mode", None, None, None),
            P(("scan", "mode"), None, None),
        ),
        check_vma=False,
    )
```

```python
import functools
import math

import jax
import jax.numpy as jnp
import ml_dtypes
import numpy as np
from jax import lax
from jax.experimental import pallas as pl
from jax.experimental.pallas import tpu as pltpu
from jax.sharding import PartitionSpec as P

MAGNITUDE_FLOOR = 0.5
OBJECT_REGULARIZER = 1.0
EPSILON = 1e-05
MESH = pl.DeviceIdType.MESH
BLOCK = 64
EXTRA = 8
VMEM_BYTES = 56 * 1024 * 1024


def dft_tables(length):
    indices = np.arange(length)
    angle = (indices[:, None] * indices[None, :] % length) * (2.0 * math.pi / length)
    cosine = np.cos(angle) / math.sqrt(length)
    sine = -np.sin(angle) / math.sqrt(length)
    right = np.block([[cosine, sine], [-sine, cosine]])
    left = np.block([[cosine, -sine], [sine, cosine]])
    found = []
    for table in (right, left):
        high = table.astype(ml_dtypes.bfloat16)
        low = (table - high.astype(np.float64)).astype(ml_dtypes.bfloat16)
        found += [high, low]
    return found


def radices(count):
    rest = count // 2
    first = 1
    while first * first * 4 <= rest:
        first *= 2
    return first, rest // first


def gather_kernel(scans, modes, probe_ref, object_ref, gathered_ref, next_ref, *sems):
    send_y, recv_y, send_c, recv_c, send_o, recv_o = sems
    s = lax.axis_index("scan")
    m = lax.axis_index("mode")
    half = probe_ref.shape[0] // 2
    core = lax.rem(s, 2)
    sibling = s + 1 - 2 * core
    rows = pl.ds(pl.multiple_of(core * half, half), half)
    barrier = pltpu.get_barrier_semaphore()
    pl.semaphore_signal(barrier, inc=1, device_id=(sibling, m), device_id_type=MESH)
    for step in range(1, modes):
        other = lax.rem(m + step, modes)
        pl.semaphore_signal(barrier, inc=1, device_id=(s, other), device_id_type=MESH)

    @pl.when(s > 0)
    def _():
        pl.semaphore_signal(barrier, inc=1, device_id=(s - 1, m), device_id_type=MESH)

    @pl.when(s < scans - 1)
    def _():
        pl.semaphore_signal(barrier, inc=1, device_id=(s + 1, m), device_id_type=MESH)

    inner = jnp.minimum(s, 1) + jnp.minimum(scans - 1 - s, 1)
    pl.semaphore_wait(barrier, modes + inner)

    def object_copy(target):
        return pltpu.make_async_remote_copy(
            src_ref=object_ref, dst_ref=next_ref, send_sem=send_o, recv_sem=recv_o,
            device_id=(target, m), device_id_type=MESH)

    def mode_copy(step):
        return pltpu.make_async_remote_copy(
            src_ref=probe_ref.at[rows], dst_ref=gathered_ref.at[m, rows],
            send_sem=send_y.at[step - 1], recv_sem=recv_y.at[step - 1],
            device_id=(s, lax.rem(m + step, modes)), device_id_type=MESH)

    def sibling_copy(step):
        source = lax.rem(m + modes - step, modes)
        return pltpu.make_async_remote_copy(
            src_ref=gathered_ref.at[source, rows], dst_ref=gathered_ref.at[source, rows],
            send_sem=send_c.at[step - 1], recv_sem=recv_c.at[step - 1],
            device_id=(sibling, m), device_id_type=MESH)

    for step in range(1, modes):
        mode_copy(step).start()

    @pl.when(s > 0)
    def _():
        object_copy(s - 1).start()

    gathered_ref[m] = probe_ref[...]
    for step in range(1, modes):
        mode_copy(step).wait_recv()
        sibling_copy(step).start()
    for step in range(1, modes):
        mode_copy(step).wait_send()
        sibling_copy(step).wait_send()
        sibling_copy(step).wait_recv()

    @pl.when(s > 0)
    def _():
        object_copy(s - 1).wait_send()

    @pl.when(s < scans - 1)
    def _():
        object_copy(s + 1).wait_recv()


def compute_kernel(modes, place_ref, coef_ref, probe_ref, own_ref, next_ref, inten_ref,
                   rh_ref, rl_ref, lh_ref, ll_ref, terms_ref, grad_ref, coef_out_ref,
                   ext_ref, wave_ref, window_ref, mixed_ref, flat_ref, tall_ref, out_ref,
                   inner_ref, weight_ref, norm_ref):
    count, length = inten_ref.shape[0], inten_ref.shape[1]
    columns = own_ref.shape[2]
    blocks = length // BLOCK
    ext_ref[:, :length] = own_ref[...]
    ext_ref[:, length:] = next_ref[...]
    terms_ref[...] = jnp.zeros_like(terms_ref)
    grad_ref[...] = jnp.zeros_like(grad_ref)

    def folded(value):
        return jnp.sum(value.reshape(BLOCK // 8, 8, length), axis=0)

    def split(value):
        high = value.astype(jnp.bfloat16)
        return high, (value - high.astype(jnp.float32)).astype(jnp.bfloat16)

    def put_flat(rows, real, imag):
        for slot, value in enumerate((real, imag)):
            high, low = split(value)
            flat_ref[rows, slot * length:(slot + 1) * length] = high
            flat_ref[rows, (2 + slot) * length:(3 + slot) * length] = low

    def dot(a, b):
        return jnp.dot(a, b, preferred_element_type=jnp.float32)

    def right_apply(high_ref, low_ref):
        size = length // 2
        for start in range(0, length, size):
            rows = slice(start, start + size)
            for slot in range(2):
                cols = slice(slot * length, (slot + 1) * length)
                part = dot(
                    jnp.concatenate([flat_ref[rows, :], flat_ref[rows, :2 * length]], axis=1),
                    jnp.concatenate([high_ref[:, cols], high_ref[:, cols], low_ref[:, cols]], axis=0))
                part_high, part_low = split(part)
                base = slot * length + start
                tall_ref[base:base + size] = part_high
                tall_ref[base + 2 * length:base + 2 * length + size] = part_low

    def left_apply(high_ref, low_ref):
        size = length // 2
        for start in range(0, 2 * length, size):
            rows = slice(start, start + size)
            out_ref[rows] = dot(
                jnp.concatenate([high_ref[rows], high_ref[rows], low_ref[rows]], axis=1),
                jnp.concatenate([tall_ref[...], tall_ref[:2 * length]], axis=0))

    norm_ref[...] = jnp.zeros_like(norm_ref)

    def norms(index, carry):
        for mode in range(modes):
            rows = pl.ds(pl.multiple_of(index * BLOCK, BLOCK), BLOCK)
            value = probe_ref[mode, rows]
            norm_ref[mode] += folded(value * value)
        return carry

    lax.fori_loop(0, 2 * blocks, norms, 0)

    def pattern(b, carry):
        top = place_ref[b, 0]
        left = place_ref[b, 1]
        back_shift = lax.rem(columns - left, columns)
        within = lax.rem(top, 8)
        top_tile = top - within
        up_shift = lax.rem(8 - within, 8)
        sublane = lax.broadcasted_iota(jnp.int32, (BLOCK // 8, 8, length), 1)
        wide = lax.broadcasted_iota(jnp.int32, (BLOCK // 8 + 1, 8, columns), 1)
        inner_ref[...] = jnp.zeros_like(inner_ref)
        weight_ref[...] = jnp.zeros_like(weight_ref)

        def first(index, carry):
            base = pl.multiple_of(index * BLOCK, BLOCK)
            rows = pl.ds(base, BLOCK)
            lower = pl.ds(pl.multiple_of(base + length, BLOCK), BLOCK)
            pr = jnp.zeros((BLOCK, length), jnp.float32)
            pi = jnp.zeros((BLOCK, length), jnp.float32)
            for mode in range(modes):
                cr, ci = coef_ref[b, 0, mode], coef_ref[b, 1, mode]
                ur, ui = probe_ref[mode, rows], probe_ref[mode, lower]
                pr = pr + cr * ur - ci * ui
                pi = pi + cr * ui + ci * ur
            window = []
            for part in range(2):
                strip = ext_ref[part, pl.ds(pl.multiple_of(top_tile + base, 8), BLOCK + 8), :]
                strip = pltpu.roll(strip, back_shift, 1)[:, :length]
                turned = pltpu.roll(strip.reshape(BLOCK // 8 + 1, 8, length), up_shift, 1)
                kept = jnp.where(sublane < 8 - within, turned[:-1], turned[1:])
                window.append(kept.reshape(BLOCK, length))
            wr, wi = window
            window_ref[rows], window_ref[lower] = wr, wi
            mixed_ref[rows], mixed_ref[lower] = pr, pi
            weight_ref[...] += folded(wr * wr + wi * wi)
            real = pr * wr - pi * wi
            imag = pr * wi + pi * wr
            wave_ref[rows], wave_ref[lower] = real, imag
            put_flat(rows, real, imag)
            return carry

        lax.fori_loop(0, blocks, first, 0)
        right_apply(rh_ref, rl_ref)
        left_apply(lh_ref, ll_ref)

        def second(index, carry):
            base = pl.multiple_of(index * BLOCK, BLOCK)
            rows = pl.ds(base, BLOCK)
            lower = pl.ds(pl.multiple_of(base + length, BLOCK), BLOCK)
            real, imag = out_ref[rows], out_ref[lower]
            power = jnp.maximum(real * real + imag * imag, MAGNITUDE_FLOOR * MAGNITUDE_FLOOR)
            factor = jnp.sqrt(inten_ref[b, rows] / power)
            put_flat(rows, real * factor, imag * factor)
            return carry

        lax.fori_loop(0, blocks, second, 0)
        right_apply(lh_ref, ll_ref)
        left_apply(rh_ref, rl_ref)

        def third(index, carry):
            base = pl.multiple_of(index * BLOCK, BLOCK)
            rows = pl.ds(base, BLOCK)
            lower = pl.ds(pl.multiple_of(base + length, BLOCK), BLOCK)
            dr = out_ref[rows] - wave_ref[rows]
            di = out_ref[lower] - wave_ref[lower]
            pr, pi = mixed_ref[rows], mixed_ref[lower]
            wr, wi = window_ref[rows], window_ref[lower]
            pieces = (pr * dr + pi * di, pr * di - pi * dr, pr * pr + pi * pi)
            for part, piece in enumerate(pieces):
                padded = jnp.concatenate(
                    [piece, jnp.zeros((BLOCK, columns - length), jnp.float32)], axis=1)
                padded = pltpu.roll(padded, left, 1).reshape(BLOCK // 8, 8, columns)
                padded = pltpu.roll(padded, within, 1)
                edge = jnp.zeros((1, 8, columns), jnp.float32)
                placed = jnp.where(
                    wide >= within,
                    jnp.concatenate([padded, edge], axis=0),
                    jnp.concatenate([edge, padded], axis=0))
                spot = pl.ds(pl.multiple_of(top_tile + base, 8), BLOCK + 8)
                terms_ref[part, spot, :] += placed.reshape(BLOCK + 8, columns)
            gr = wr * dr + wi * di
            gi = wr * di - wi * dr
            for mode in range(modes):
                cr, ci = coef_ref[b, 0, mode], coef_ref[b, 1, mode]
                ur, ui = probe_ref[mode, rows], probe_ref[mode, lower]
                shifted = pl.ds(pl.multiple_of(base + EXTRA, 8), BLOCK)
                grad_ref[0, mode, shifted] += cr * gr + ci * gi
                grad_ref[1, mode, shifted] += cr * gi - ci * gr
                inner_ref[mode, 0] += folded(ur * gr + ui * gi)
                inner_ref[mode, 1] += folded(ur * gi - ui * gr)
            return carry

        lax.fori_loop(0, blocks, third, 0)

        def total(value):
            return jnp.sum(jnp.sum(value, axis=1, keepdims=True), axis=0, keepdims=True)

        weight = total(weight_ref[...]) * (1.0 / (length * length))
        lanes = lax.broadcasted_iota(jnp.int32, (1, modes), 1)
        found = [jnp.zeros((1, modes), jnp.float32)] * 2
        for mode in range(modes):
            cr, ci = coef_ref[b, 0, mode], coef_ref[b, 1, mode]
            denominator = total(norm_ref[mode]) * weight + EPSILON
            for part, c in enumerate((cr, ci)):
                value = c + total(inner_ref[mode, part]) / denominator
                found[part] = jnp.where(lanes == mode, value, found[part])
            share = jnp.broadcast_to((cr * cr + ci * ci) * weight, (1, length))
            for part in range(2):
                grad_ref[part, mode, :EXTRA] += jnp.broadcast_to(share, (EXTRA, length))
        coef_out_ref[b] = jnp.concatenate(found, axis=0)
        return carry

    lax.fori_loop(0, count, pattern, 0)


def reduce_kernel(scans, modes, terms_ref, grad_ref, object_ref, probe_ref,
                  object_out_ref, probe_out_ref,
                  core_in, mode_in, stage1, in1, stage2, in2, weight_ref, shift_in, stage_n, numer_in,
                  send_g, recv_g, send_y, recv_y, send_1, recv_1, send_2, recv_2,
                  back_s0, back_r0, back_s1, back_r1, back_s2, back_r2,
                  send_s, recv_s, send_n, recv_n, send_a, recv_a):
    s = lax.axis_index("scan")
    m = lax.axis_index("mode")
    r1, r2 = radices(scans)
    length = object_ref.shape[1]
    d0 = lax.rem(s, 2)
    d1 = lax.rem(s // 2, r1)
    d2 = s // (2 * r1)
    rows_m = length // modes
    sibling = (s + 1 - 2 * d0, m)

    def peer1(step):
        return ((d2 * r1 + lax.rem(d1 + step, r1)) * 2 + d0, m)

    def peer2(step):
        return ((lax.rem(d2 + step, r2) * r1 + d1) * 2 + d0, m)

    def peer_m(step):
        return (s, lax.rem(m + step, modes))

    peers = [sibling] + [peer1(i) for i in range(1, r1)] + [peer2(i) for i in range(1, r2)]
    peers += [peer_m(i) for i in range(1, modes)]
    barrier = pltpu.get_barrier_semaphore()
    for peer in peers:
        pl.semaphore_signal(barrier, inc=1, device_id=peer, device_id_type=MESH)

    @pl.when(s > 0)
    def _():
        pl.semaphore_signal(barrier, inc=1, device_id=(s - 1, m), device_id_type=MESH)

    @pl.when(s < scans - 1)
    def _():
        pl.semaphore_signal(barrier, inc=1, device_id=(s + 1, m), device_id_type=MESH)

    inner = jnp.minimum(s, 1) + jnp.minimum(scans - 1 - s, 1)
    pl.semaphore_wait(barrier, len(peers) + inner)

    def remote(src, dst, send, recv, peer):
        return pltpu.make_async_remote_copy(
            src_ref=src, dst_ref=dst, send_sem=send, recv_sem=recv,
            device_id=peer, device_id_type=MESH)

    parts = send_s.shape[1]
    rows_c = rows_m // parts
    pending = []

    def begin(*arguments):
        copy = remote(*arguments)
        copy.start()
        pending.append(copy)
        return copy

    def chunk(owner, part):
        return pl.ds(pl.multiple_of(owner * rows_m + part * rows_c, rows_c), rows_c)

    def shift_copy(step, part, target):
        rows = chunk(lax.rem(m + step, modes), part)
        away = chunk(lax.rem(m + step, modes) + modes, part)
        return remote(terms_ref.at[:, away], shift_in.at[:, rows],
                      send_s.at[step - 1, part], recv_s.at[step - 1, part], (target, m))

    def shift_start(steps):
        @pl.when(s < scans - 1)
        def _():
            for step in steps:
                for part in range(parts):
                    shift_copy(step, part, s + 1).start()

    def shift_wait(step, part):
        @pl.when(s > 0)
        def _():
            shift_copy(step, part, s - 1).wait_recv()

    def gradient(q):
        size = length // groups
        extra = EXTRA if q == 0 else 0
        rows = pl.ds(0 if q == 0 else EXTRA + q * size, size + extra)
        c1, c2 = size // r1, size // (r1 * r2)
        core = begin(grad_ref.at[1 - d0, :, rows], core_in.at[:, rows],
                     send_g.at[q], recv_g.at[q], sibling)
        yield
        core.wait_recv()
        copies = []
        for step in range(1, modes):
            owner = lax.rem(m + step, modes)
            core_in[owner, rows] = core_in[owner, rows] + grad_ref[d0, owner, rows]
            copies.append(begin(core_in.at[owner, rows], mode_in.at[step - 1, rows],
                                send_y.at[q, step - 1], recv_y.at[q, step - 1], peer_m(step)))
        yield
        total = core_in[m, rows] + grad_ref[d0, m, rows]
        for step in range(1, modes):
            copies[step - 1].wait_recv()
            total = total + mode_in[step - 1, rows]
        levels = ((r1, c1, d1, stage1, in1, send_1, recv_1, peer1),
                  (r2, c2, d2, stage2, in2, send_2, recv_2, peer2))
        for radix, c, digit, stage, landed, send, recv, peer in levels:
            for index in range(radix):
                if extra:
                    stage[q, index, :extra] = total[:extra]
                stage[q, index, extra:extra + c] = total[extra + index * c:extra + (index + 1) * c]
            held = pl.ds(0, c + extra)
            copies = []
            for step in range(1, radix):
                copies.append(begin(stage.at[q, lax.rem(digit + step, radix), held],
                                    landed.at[q, step - 1, held],
                                    send.at[q, step - 1], recv.at[q, step - 1], peer(step)))
            yield
            total = stage[q, digit, held]
            for step in range(1, radix):
                copies[step - 1].wait_recv()
                total = total + landed[q, step - 1, held]
        if extra:
            weight_ref[...] = total[:extra]
        start0 = d0 * length + q * size
        start1 = start0 + d1 * c1
        start2 = start1 + d2 * c2
        block0 = pl.ds(pl.multiple_of(start0, size), size)
        block1 = pl.ds(pl.multiple_of(start1, c1), c1)
        block2 = pl.ds(pl.multiple_of(start2, c2), c2)
        probe_out_ref[block2] = probe_ref[block2] + total[extra:] / weight_ref[0:1]
        for block, radix, send, recv, peer in ((block2, r2, back_s2, back_r2, peer2),
                                               (block1, r1, back_s1, back_r1, peer1),
                                               (block0, 2, back_s0, back_r0, lambda step: sibling)):
            copies = []
            for step in range(1, radix):
                copies.append(begin(probe_out_ref.at[block], probe_out_ref.at[block],
                                    send.at[q, step - 1], recv.at[q, step - 1], peer(step)))
            yield
            for copy in copies:
                copy.wait_recv()
        yield

    def terms():
        copies = {}
        for part in range(parts):
            for step in range(1, modes):
                rows = chunk(lax.rem(m + step, modes), part)
                shift_wait(step, part)
                stage_n[step - 1, part] = terms_ref[:, rows] + shift_in[:, rows]
                copies[step, part] = begin(
                    stage_n.at[step - 1, part], numer_in.at[step - 1, part],
                    send_n.at[step - 1, part], recv_n.at[step - 1, part], peer_m(step))
            if part == parts - 1:
                shift_start([modes])
            yield
        back = []
        for part in range(parts):
            rows = chunk(m, part)
            shift_wait(modes, part)
            found = [terms_ref[k, rows] + shift_in[k, rows] for k in range(3)]
            for step in range(1, modes):
                copies[step, part].wait_recv()
                found = [found[k] + numer_in[step - 1, part, k] for k in range(3)]
            scale = found[2] + OBJECT_REGULARIZER
            for k in range(2):
                object_out_ref[k, rows] = object_ref[k, rows] + found[k] / scale
            for step in range(1, modes):
                back.append(begin(object_out_ref.at[:, rows], object_out_ref.at[:, rows],
                                  send_a.at[step - 1, part], recv_a.at[step - 1, part], peer_m(step)))
            yield
        for copy in back:
            copy.wait_recv()
        yield

    groups = send_g.shape[0]
    chains = [gradient(q) for q in range(groups)]
    objects = terms()

    def advance():
        for chain in chains:
            next(chain)

    advance()
    shift_start(range(1, modes))

    @pl.when(s == 0)
    def _():
        shift_in[...] = jnp.zeros_like(shift_in)

    advance()
    next(objects)
    next(chains[0])
    for _ in range(parts - 1):
        next(objects)
    for chain in chains[1:]:
        next(chain)
    advance()
    for index in range(parts):
        next(objects)
        if index < 2:
            advance()
    for _ in range(2 - min(parts, 2)):
        advance()
    advance()
    advance()
    next(objects)

    @pl.when(s < scans - 1)
    def _():
        for step in range(1, modes + 1):
            for part in range(parts):
                shift_copy(step, part, s + 1).wait_send()

    for copy in pending:
        copy.wait_send()


def on_device(scans, modes, object_field, eigen_probes, coeffs, intensities, positions):
    length = eigen_probes.shape[2]
    columns = object_field.shape[2]
    f32 = jnp.float32
    vmem = pl.BlockSpec(memory_space=pltpu.VMEM)
    smem = pl.BlockSpec(memory_space=pltpu.SMEM)
    dma = pltpu.SemaphoreType.DMA
    probe = eigen_probes.reshape(2 * length, length)
    others = max(modes - 1, 1)
    r1, r2 = radices(scans)
    groups = 2 if length // (r1 * r2) >= 16 else 1
    b1, b2 = length // (r1 * groups), length // (r1 * r2 * groups)
    parts = 2 if modes == 2 else 1
    rows_c = length // (modes * parts)
    gathered, following = pl.pallas_call(
        functools.partial(gather_kernel, scans, modes),
        out_shape=(
            jax.ShapeDtypeStruct((modes, 2 * length, length), f32),
            jax.ShapeDtypeStruct(object_field.shape, f32),
        ),
        in_specs=[vmem] * 2,
        out_specs=(vmem, vmem),
        scratch_shapes=[dma((others,))] * 4 + [dma, dma],
        compiler_params=pltpu.CompilerParams(
            collective_id=0, has_side_effects=True, vmem_limit_bytes=VMEM_BYTES),
        name="gather_probes",
    )(probe, object_field)
    row_start = positions[:, 0] - lax.axis_index("scan") * length
    place = jnp.stack([row_start, positions[:, 1]], axis=1)
    tables = [jnp.asarray(table) for table in dft_tables(length)]
    terms, grads, coeffs_new = pl.pallas_call(
        functools.partial(compute_kernel, modes),
        out_shape=(
            jax.ShapeDtypeStruct((3, 2 * length, columns), f32),
            jax.ShapeDtypeStruct((2, modes, length + EXTRA, length), f32),
            jax.ShapeDtypeStruct(coeffs.shape, f32),
        ),
        in_specs=[smem, smem] + [vmem] * 8,
        out_specs=(vmem, vmem, vmem),
        scratch_shapes=[
            pltpu.VMEM((2, 2 * length, columns), f32),
            pltpu.VMEM((2 * length, length), f32),
            pltpu.VMEM((2 * length, length), f32),
            pltpu.VMEM((2 * length, length), f32),
            pltpu.VMEM((length, 4 * length), jnp.bfloat16),
            pltpu.VMEM((4 * length, length), jnp.bfloat16),
            pltpu.VMEM((2 * length, length), f32),
            pltpu.VMEM((modes, 2, 8, length), f32),
            pltpu.VMEM((8, length), f32),
            pltpu.VMEM((modes, 8, length), f32),
        ],
        compiler_params=pltpu.CompilerParams(vmem_limit_bytes=VMEM_BYTES),
        name="local_terms",
    )(place, coeffs, gathered, object_field, following, intensities, *tables)
    object_new, probes_new = pl.pallas_call(
        functools.partial(reduce_kernel, scans, modes),
        out_shape=(
            jax.ShapeDtypeStruct(object_field.shape, f32),
            jax.ShapeDtypeStruct((2 * length, length), f32),
        ),
        in_specs=[vmem] * 4,
        out_specs=(vmem, vmem),
        scratch_shapes=[
            pltpu.VMEM((modes, length + EXTRA, length), f32),
            pltpu.VMEM((others, length + EXTRA, length), f32),
            pltpu.VMEM((groups, r1, b1 + EXTRA, length), f32),
            pltpu.VMEM((groups, max(r1 - 1, 1), b1 + EXTRA, length), f32),
            pltpu.VMEM((groups, r2, b2 + EXTRA, length), f32),
            pltpu.VMEM((groups, max(r2 - 1, 1), b2 + EXTRA, length), f32),
            pltpu.VMEM((EXTRA, length), f32),
            pltpu.VMEM((3, length, columns), f32),
            pltpu.VMEM((others, parts, 3, rows_c, columns), f32),
            pltpu.VMEM((others, parts, 3, rows_c, columns), f32),
            dma((groups,)), dma((groups,)),
            dma((groups, others)), dma((groups, others)),
            dma((groups, max(r1 - 1, 1))), dma((groups, max(r1 - 1, 1))),
            dma((groups, max(r2 - 1, 1))), dma((groups, max(r2 - 1, 1))),
            dma((groups, 1)), dma((groups, 1)),
            dma((groups, max(r1 - 1, 1))), dma((groups, max(r1 - 1, 1))),
            dma((groups, max(r2 - 1, 1))), dma((groups, max(r2 - 1, 1))),
            dma((modes, parts)), dma((modes, parts)),
            dma((others, parts)), dma((others, parts)),
            dma((others, parts)), dma((others, parts)),
        ],
        compiler_params=pltpu.CompilerParams(
            collective_id=1, has_side_effects=True, vmem_limit_bytes=VMEM_BYTES),
        name="reduce_terms",
    )(terms, grads, object_field, probe)
    return object_new, probes_new.reshape(eigen_probes.shape), coeffs_new


def solution(mesh):
    return jax.shard_map(
        functools.partial(on_device, mesh.shape["scan"], mesh.shape["mode"]),
        mesh=mesh,
        in_specs=(
            P(None, "scan", None),
            P("mode", None, None, None),
            P(("scan", "mode"), None, None),
            P(("scan", "mode"), None, None),
            P(("scan", "mode"), None),
        ),
        out_specs=(
            P(None, "scan", None),
            P("mode", None, None, None),
            P(("scan", "mode"), None, None),
        ),
        check_vma=False,
    )
```

```python
import functools
import math

import jax
import jax.numpy as jnp
import ml_dtypes
import numpy as np
from jax import lax
from jax.experimental import pallas as pl
from jax.experimental.pallas import tpu as pltpu
from jax.sharding import PartitionSpec as P

MAGNITUDE_FLOOR = 0.5
OBJECT_REGULARIZER = 1.0
EPSILON = 1e-05
MESH = pl.DeviceIdType.MESH
BLOCK = 64
EXTRA = 8
VMEM_BYTES = 56 * 1024 * 1024


def dft_tables(length):
    indices = np.arange(length)
    angle = (indices[:, None] * indices[None, :] % length) * (2.0 * math.pi / length)
    cosine = np.cos(angle) / math.sqrt(length)
    sine = -np.sin(angle) / math.sqrt(length)
    right = np.block([[cosine, sine], [-sine, cosine]])
    left = np.block([[cosine, -sine], [sine, cosine]])
    found = []
    for table in (right, left):
        high = table.astype(ml_dtypes.bfloat16)
        low = (table - high.astype(np.float64)).astype(ml_dtypes.bfloat16)
        found += [high, low]
    return found


def radices(count):
    rest = count // 2
    first = 1
    while first * first * 4 <= rest:
        first *= 2
    return first, rest // first


def gather_kernel(scans, modes, probe_ref, object_ref, gathered_ref, next_ref, *sems):
    send_y, recv_y, send_c, recv_c, send_o, recv_o = sems
    s = lax.axis_index("scan")
    m = lax.axis_index("mode")
    half = probe_ref.shape[0] // 2
    core = lax.rem(s, 2)
    sibling = s + 1 - 2 * core
    rows = pl.ds(pl.multiple_of(core * half, half), half)
    barrier = pltpu.get_barrier_semaphore()
    pl.semaphore_signal(barrier, inc=1, device_id=(sibling, m), device_id_type=MESH)
    for step in range(1, modes):
        other = lax.rem(m + step, modes)
        pl.semaphore_signal(barrier, inc=1, device_id=(s, other), device_id_type=MESH)

    @pl.when(s > 0)
    def _():
        pl.semaphore_signal(barrier, inc=1, device_id=(s - 1, m), device_id_type=MESH)

    @pl.when(s < scans - 1)
    def _():
        pl.semaphore_signal(barrier, inc=1, device_id=(s + 1, m), device_id_type=MESH)

    inner = jnp.minimum(s, 1) + jnp.minimum(scans - 1 - s, 1)
    pl.semaphore_wait(barrier, modes + inner)

    def object_copy(target):
        return pltpu.make_async_remote_copy(
            src_ref=object_ref, dst_ref=next_ref, send_sem=send_o, recv_sem=recv_o,
            device_id=(target, m), device_id_type=MESH)

    def mode_copy(step):
        return pltpu.make_async_remote_copy(
            src_ref=probe_ref.at[rows], dst_ref=gathered_ref.at[m, rows],
            send_sem=send_y.at[step - 1], recv_sem=recv_y.at[step - 1],
            device_id=(s, lax.rem(m + step, modes)), device_id_type=MESH)

    def sibling_copy(step):
        source = lax.rem(m + modes - step, modes)
        return pltpu.make_async_remote_copy(
            src_ref=gathered_ref.at[source, rows], dst_ref=gathered_ref.at[source, rows],
            send_sem=send_c.at[step - 1], recv_sem=recv_c.at[step - 1],
            device_id=(sibling, m), device_id_type=MESH)

    @pl.when(s > 0)
    def _():
        object_copy(s - 1).start()

    for step in range(1, modes):
        mode_copy(step).start()

    gathered_ref[m] = probe_ref[...]
    for step in range(1, modes):
        mode_copy(step).wait_recv()
        sibling_copy(step).start()
    for step in range(1, modes):
        mode_copy(step).wait_send()
        sibling_copy(step).wait_send()
        sibling_copy(step).wait_recv()

    @pl.when(s > 0)
    def _():
        object_copy(s - 1).wait_send()

    @pl.when(s < scans - 1)
    def _():
        object_copy(s + 1).wait_recv()


def compute_kernel(modes, place_ref, coef_ref, probe_ref, own_ref, next_ref, inten_ref,
                   rh_ref, rl_ref, lh_ref, ll_ref, terms_ref, grad_ref, coef_out_ref,
                   ext_ref, wave_ref, window_ref, mixed_ref, flat_ref, tall_ref, out_ref,
                   inner_ref, weight_ref, norm_ref):
    count, length = inten_ref.shape[0], inten_ref.shape[1]
    columns = own_ref.shape[2]
    blocks = length // BLOCK
    ext_ref[:, :length] = own_ref[...]
    ext_ref[:, length:] = next_ref[...]
    terms_ref[...] = jnp.zeros_like(terms_ref)
    grad_ref[...] = jnp.zeros_like(grad_ref)

    def folded(value):
        return jnp.sum(value.reshape(BLOCK // 8, 8, length), axis=0)

    def split(value):
        high = value.astype(jnp.bfloat16)
        return high, (value - high.astype(jnp.float32)).astype(jnp.bfloat16)

    def put_flat(rows, real, imag):
        for slot, value in enumerate((real, imag)):
            high, low = split(value)
            flat_ref[rows, slot * length:(slot + 1) * length] = high
            flat_ref[rows, (2 + slot) * length:(3 + slot) * length] = low

    def dot(a, b):
        return jnp.dot(a, b, preferred_element_type=jnp.float32)

    def right_apply(high_ref, low_ref):
        size = length // 2
        for start in range(0, length, size):
            rows = slice(start, start + size)
            for slot in range(2):
                cols = slice(slot * length, (slot + 1) * length)
                part = dot(
                    jnp.concatenate([flat_ref[rows, :], flat_ref[rows, :2 * length]], axis=1),
                    jnp.concatenate([high_ref[:, cols], high_ref[:, cols], low_ref[:, cols]], axis=0))
                part_high, part_low = split(part)
                base = slot * length + start
                tall_ref[base:base + size] = part_high
                tall_ref[base + 2 * length:base + 2 * length + size] = part_low

    def left_apply(high_ref, low_ref):
        size = length // 2
        for start in range(0, 2 * length, size):
            rows = slice(start, start + size)
            out_ref[rows] = dot(
                jnp.concatenate([high_ref[rows], high_ref[rows], low_ref[rows]], axis=1),
                jnp.concatenate([tall_ref[...], tall_ref[:2 * length]], axis=0))

    norm_ref[...] = jnp.zeros_like(norm_ref)

    def norms(index, carry):
        for mode in range(modes):
            rows = pl.ds(pl.multiple_of(index * BLOCK, BLOCK), BLOCK)
            value = probe_ref[mode, rows]
            norm_ref[mode] += folded(value * value)
        return carry

    lax.fori_loop(0, 2 * blocks, norms, 0)

    def pattern(b, carry):
        top = place_ref[b, 0] - lax.axis_index("scan") * length
        left = place_ref[b, 1]
        back_shift = lax.rem(columns - left, columns)
        within = lax.rem(top, 8)
        top_tile = top - within
        up_shift = lax.rem(8 - within, 8)
        sublane = lax.broadcasted_iota(jnp.int32, (BLOCK // 8, 8, length), 1)
        wide = lax.broadcasted_iota(jnp.int32, (BLOCK // 8 + 1, 8, columns), 1)
        inner_ref[...] = jnp.zeros_like(inner_ref)
        weight_ref[...] = jnp.zeros_like(weight_ref)

        def first(index, carry):
            base = pl.multiple_of(index * BLOCK, BLOCK)
            rows = pl.ds(base, BLOCK)
            lower = pl.ds(pl.multiple_of(base + length, BLOCK), BLOCK)
            pr = jnp.zeros((BLOCK, length), jnp.float32)
            pi = jnp.zeros((BLOCK, length), jnp.float32)
            for mode in range(modes):
                cr, ci = coef_ref[b, 0, mode], coef_ref[b, 1, mode]
                ur, ui = probe_ref[mode, rows], probe_ref[mode, lower]
                pr = pr + cr * ur - ci * ui
                pi = pi + cr * ui + ci * ur
            window = []
            for part in range(2):
                strip = ext_ref[part, pl.ds(pl.multiple_of(top_tile + base, 8), BLOCK + 8), :]
                strip = pltpu.roll(strip, back_shift, 1)[:, :length]
                turned = pltpu.roll(strip.reshape(BLOCK // 8 + 1, 8, length), up_shift, 1)
                kept = jnp.where(sublane < 8 - within, turned[:-1], turned[1:])
                window.append(kept.reshape(BLOCK, length))
            wr, wi = window
            window_ref[rows], window_ref[lower] = wr, wi
            mixed_ref[rows], mixed_ref[lower] = pr, pi
            weight_ref[...] += folded(wr * wr + wi * wi)
            real = pr * wr - pi * wi
            imag = pr * wi + pi * wr
            wave_ref[rows], wave_ref[lower] = real, imag
            put_flat(rows, real, imag)
            return carry

        lax.fori_loop(0, blocks, first, 0)
        right_apply(rh_ref, rl_ref)
        left_apply(lh_ref, ll_ref)

        def second(index, carry):
            base = pl.multiple_of(index * BLOCK, BLOCK)
            rows = pl.ds(base, BLOCK)
            lower = pl.ds(pl.multiple_of(base + length, BLOCK), BLOCK)
            real, imag = out_ref[rows], out_ref[lower]
            power = jnp.maximum(real * real + imag * imag, MAGNITUDE_FLOOR * MAGNITUDE_FLOOR)
            factor = jnp.sqrt(inten_ref[b, rows] / power)
            put_flat(rows, real * factor, imag * factor)
            return carry

        lax.fori_loop(0, blocks, second, 0)
        right_apply(lh_ref, ll_ref)
        left_apply(rh_ref, rl_ref)

        def third(index, carry):
            base = pl.multiple_of(index * BLOCK, BLOCK)
            rows = pl.ds(base, BLOCK)
            lower = pl.ds(pl.multiple_of(base + length, BLOCK), BLOCK)
            dr = out_ref[rows] - wave_ref[rows]
            di = out_ref[lower] - wave_ref[lower]
            pr, pi = mixed_ref[rows], mixed_ref[lower]
            wr, wi = window_ref[rows], window_ref[lower]
            pieces = (pr * dr + pi * di, pr * di - pi * dr, pr * pr + pi * pi)
            for part, piece in enumerate(pieces):
                padded = jnp.concatenate(
                    [piece, jnp.zeros((BLOCK, columns - length), jnp.float32)], axis=1)
                padded = pltpu.roll(padded, left, 1).reshape(BLOCK // 8, 8, columns)
                padded = pltpu.roll(padded, within, 1)
                edge = jnp.zeros((1, 8, columns), jnp.float32)
                placed = jnp.where(
                    wide >= within,
                    jnp.concatenate([padded, edge], axis=0),
                    jnp.concatenate([edge, padded], axis=0))
                spot = pl.ds(pl.multiple_of(top_tile + base, 8), BLOCK + 8)
                terms_ref[part, spot, :] += placed.reshape(BLOCK + 8, columns)
            gr = wr * dr + wi * di
            gi = wr * di - wi * dr
            for mode in range(modes):
                cr, ci = coef_ref[b, 0, mode], coef_ref[b, 1, mode]
                ur, ui = probe_ref[mode, rows], probe_ref[mode, lower]
                shifted = pl.ds(pl.multiple_of(base + EXTRA, 8), BLOCK)
                grad_ref[0, mode, shifted] += cr * gr + ci * gi
                grad_ref[1, mode, shifted] += cr * gi - ci * gr
                inner_ref[mode, 0] += folded(ur * gr + ui * gi)
                inner_ref[mode, 1] += folded(ur * gi - ui * gr)
            return carry

        lax.fori_loop(0, blocks, third, 0)

        def total(value):
            return jnp.sum(jnp.sum(value, axis=1, keepdims=True), axis=0, keepdims=True)

        weight = total(weight_ref[...]) * (1.0 / (length * length))
        lanes = lax.broadcasted_iota(jnp.int32, (1, modes), 1)
        found = [jnp.zeros((1, modes), jnp.float32)] * 2
        for mode in range(modes):
            cr, ci = coef_ref[b, 0, mode], coef_ref[b, 1, mode]
            denominator = total(norm_ref[mode]) * weight + EPSILON
            for part, c in enumerate((cr, ci)):
                value = c + total(inner_ref[mode, part]) / denominator
                found[part] = jnp.where(lanes == mode, value, found[part])
            share = jnp.broadcast_to((cr * cr + ci * ci) * weight, (1, length))
            for part in range(2):
                grad_ref[part, mode, :EXTRA] += jnp.broadcast_to(share, (EXTRA, length))
        coef_out_ref[b] = jnp.concatenate(found, axis=0)
        return carry

    lax.fori_loop(0, count, pattern, 0)


def reduce_kernel(scans, modes, terms_ref, grad_ref,
                  object_out_ref, probe_out_ref,
                  core_in, mode_in, stage1, in1, stage2, in2, weight_ref, shift_in, stage_n, numer_in,
                  send_g, recv_g, send_y, recv_y, send_1, recv_1, send_2, recv_2,
                  back_s0, back_r0, back_s1, back_r1, back_s2, back_r2,
                  send_s, recv_s, send_n, recv_n, send_a, recv_a):
    s = lax.axis_index("scan")
    m = lax.axis_index("mode")
    r1, r2 = radices(scans)
    length = terms_ref.shape[1] // 2
    d0 = lax.rem(s, 2)
    d1 = lax.rem(s // 2, r1)
    d2 = s // (2 * r1)
    rows_m = length // modes
    sibling = (s + 1 - 2 * d0, m)

    def peer1(step):
        return ((d2 * r1 + lax.rem(d1 + step, r1)) * 2 + d0, m)

    def peer2(step):
        return ((lax.rem(d2 + step, r2) * r1 + d1) * 2 + d0, m)

    def peer_m(step):
        return (s, lax.rem(m + step, modes))

    peers = [sibling] + [peer1(i) for i in range(1, r1)] + [peer2(i) for i in range(1, r2)]
    peers += [peer_m(i) for i in range(1, modes)]
    barrier = pltpu.get_barrier_semaphore()
    for peer in peers:
        pl.semaphore_signal(barrier, inc=1, device_id=peer, device_id_type=MESH)

    @pl.when(s > 0)
    def _():
        pl.semaphore_signal(barrier, inc=1, device_id=(s - 1, m), device_id_type=MESH)

    @pl.when(s < scans - 1)
    def _():
        pl.semaphore_signal(barrier, inc=1, device_id=(s + 1, m), device_id_type=MESH)

    inner = jnp.minimum(s, 1) + jnp.minimum(scans - 1 - s, 1)
    pl.semaphore_wait(barrier, len(peers) + inner)

    def remote(src, dst, send, recv, peer):
        return pltpu.make_async_remote_copy(
            src_ref=src, dst_ref=dst, send_sem=send, recv_sem=recv,
            device_id=peer, device_id_type=MESH)

    parts = send_s.shape[1]
    rows_c = rows_m // parts
    pending = []

    def begin(*arguments):
        copy = remote(*arguments)
        copy.start()
        pending.append(copy)
        return copy

    def chunk(owner, part):
        return pl.ds(pl.multiple_of(owner * rows_m + part * rows_c, rows_c), rows_c)

    def shift_copy(step, part, target):
        rows = chunk(lax.rem(m + step, modes), part)
        away = chunk(lax.rem(m + step, modes) + modes, part)
        return remote(terms_ref.at[:, away], shift_in.at[:, rows],
                      send_s.at[step - 1, part], recv_s.at[step - 1, part], (target, m))

    def shift_start(steps):
        @pl.when(s < scans - 1)
        def _():
            for step in steps:
                for part in range(parts):
                    shift_copy(step, part, s + 1).start()

    def shift_wait(step, part):
        @pl.when(s > 0)
        def _():
            shift_copy(step, part, s - 1).wait_recv()

    def gradient(q):
        size = length // groups
        extra = EXTRA if q == 0 else 0
        rows = pl.ds(0 if q == 0 else EXTRA + q * size, size + extra)
        c1, c2 = size // r1, size // (r1 * r2)
        core = begin(grad_ref.at[1 - d0, :, rows], core_in.at[:, rows],
                     send_g.at[q], recv_g.at[q], sibling)
        yield
        core.wait_recv()
        copies = []
        for step in range(1, modes):
            owner = lax.rem(m + step, modes)
            core_in[owner, rows] = core_in[owner, rows] + grad_ref[d0, owner, rows]
            copies.append(begin(core_in.at[owner, rows], mode_in.at[step - 1, rows],
                                send_y.at[q, step - 1], recv_y.at[q, step - 1], peer_m(step)))
        yield
        total = core_in[m, rows] + grad_ref[d0, m, rows]
        for step in range(1, modes):
            copies[step - 1].wait_recv()
            total = total + mode_in[step - 1, rows]
        levels = ((r1, c1, d1, stage1, in1, send_1, recv_1, peer1),
                  (r2, c2, d2, stage2, in2, send_2, recv_2, peer2))
        for radix, c, digit, stage, landed, send, recv, peer in levels:
            for index in range(radix):
                if extra:
                    stage[q, index, :extra] = total[:extra]
                stage[q, index, extra:extra + c] = total[extra + index * c:extra + (index + 1) * c]
            held = pl.ds(0, c + extra)
            copies = []
            for step in range(1, radix):
                copies.append(begin(stage.at[q, lax.rem(digit + step, radix), held],
                                    landed.at[q, step - 1, held],
                                    send.at[q, step - 1], recv.at[q, step - 1], peer(step)))
            yield
            total = stage[q, digit, held]
            for step in range(1, radix):
                copies[step - 1].wait_recv()
                total = total + landed[q, step - 1, held]
        if extra:
            weight_ref[...] = total[:extra]
        start0 = d0 * length + q * size
        start1 = start0 + d1 * c1
        start2 = start1 + d2 * c2
        block0 = pl.ds(pl.multiple_of(start0, size), size)
        block1 = pl.ds(pl.multiple_of(start1, c1), c1)
        block2 = pl.ds(pl.multiple_of(start2, c2), c2)
        probe_out_ref[block2] = total[extra:] / weight_ref[0:1]
        for block, radix, send, recv, peer in ((block2, r2, back_s2, back_r2, peer2),
                                               (block1, r1, back_s1, back_r1, peer1),
                                               (block0, 2, back_s0, back_r0, lambda step: sibling)):
            copies = []
            for step in range(1, radix):
                copies.append(begin(probe_out_ref.at[block], probe_out_ref.at[block],
                                    send.at[q, step - 1], recv.at[q, step - 1], peer(step)))
            yield
            for copy in copies:
                copy.wait_recv()
        yield

    def terms():
        copies = {}
        for part in range(parts):
            for step in range(1, modes):
                rows = chunk(lax.rem(m + step, modes), part)
                shift_wait(step, part)
                stage_n[step - 1, part] = terms_ref[:, rows] + shift_in[:, rows]
                copies[step, part] = begin(
                    stage_n.at[step - 1, part], numer_in.at[step - 1, part],
                    send_n.at[step - 1, part], recv_n.at[step - 1, part], peer_m(step))
            if part == parts - 1:
                shift_start([modes])
            yield
        back = []
        for part in range(parts):
            rows = chunk(m, part)
            shift_wait(modes, part)
            found = [terms_ref[k, rows] + shift_in[k, rows] for k in range(3)]
            for step in range(1, modes):
                copies[step, part].wait_recv()
                found = [found[k] + numer_in[step - 1, part, k] for k in range(3)]
            scale = found[2] + OBJECT_REGULARIZER
            for k in range(2):
                object_out_ref[k, rows] = found[k] / scale
            for step in range(1, modes):
                back.append(begin(object_out_ref.at[:, rows], object_out_ref.at[:, rows],
                                  send_a.at[step - 1, part], recv_a.at[step - 1, part], peer_m(step)))
            yield
        for copy in back:
            copy.wait_recv()
        yield

    groups = send_g.shape[0]
    chains = [gradient(q) for q in range(groups)]
    objects = terms()

    def advance():
        for chain in chains:
            next(chain)

    advance()
    shift_start(range(1, modes))

    @pl.when(s == 0)
    def _():
        shift_in[...] = jnp.zeros_like(shift_in)

    advance()
    next(objects)
    next(chains[0])
    for _ in range(parts - 1):
        next(objects)
    for chain in chains[1:]:
        next(chain)
    advance()
    for index in range(parts):
        next(objects)
        if index < 2:
            advance()
    for _ in range(2 - min(parts, 2)):
        advance()
    advance()
    advance()
    next(objects)

    @pl.when(s < scans - 1)
    def _():
        for step in range(1, modes + 1):
            for part in range(parts):
                shift_copy(step, part, s + 1).wait_send()

    for copy in pending:
        copy.wait_send()


def on_device(scans, modes, object_field, eigen_probes, coeffs, intensities, positions):
    length = eigen_probes.shape[2]
    columns = object_field.shape[2]
    f32 = jnp.float32
    vmem = pl.BlockSpec(memory_space=pltpu.VMEM)
    smem = pl.BlockSpec(memory_space=pltpu.SMEM)
    dma = pltpu.SemaphoreType.DMA
    probe = eigen_probes.reshape(2 * length, length)
    others = max(modes - 1, 1)
    r1, r2 = radices(scans)
    groups = 2 if length // (r1 * r2) >= 16 else 1
    b1, b2 = length // (r1 * groups), length // (r1 * r2 * groups)
    parts = 2 if modes == 2 else 1
    rows_c = length // (modes * parts)
    gathered, following = pl.pallas_call(
        functools.partial(gather_kernel, scans, modes),
        out_shape=(
            jax.ShapeDtypeStruct((modes, 2 * length, length), f32),
            jax.ShapeDtypeStruct(object_field.shape, f32),
        ),
        in_specs=[vmem] * 2,
        out_specs=(vmem, vmem),
        scratch_shapes=[dma((others,))] * 4 + [dma, dma],
        compiler_params=pltpu.CompilerParams(
            collective_id=0, has_side_effects=True, vmem_limit_bytes=VMEM_BYTES),
        name="gather_probes",
    )(probe, object_field)
    tables = [jnp.asarray(table) for table in dft_tables(length)]
    terms, grads, coeffs_new = pl.pallas_call(
        functools.partial(compute_kernel, modes),
        out_shape=(
            jax.ShapeDtypeStruct((3, 2 * length, columns), f32),
            jax.ShapeDtypeStruct((2, modes, length + EXTRA, length), f32),
            jax.ShapeDtypeStruct(coeffs.shape, f32),
        ),
        in_specs=[smem, smem] + [vmem] * 8,
        out_specs=(vmem, vmem, vmem),
        scratch_shapes=[
            pltpu.VMEM((2, 2 * length, columns), f32),
            pltpu.VMEM((2 * length, length), f32),
            pltpu.VMEM((2 * length, length), f32),
            pltpu.VMEM((2 * length, length), f32),
            pltpu.VMEM((length, 4 * length), jnp.bfloat16),
            pltpu.VMEM((4 * length, length), jnp.bfloat16),
            pltpu.VMEM((2 * length, length), f32),
            pltpu.VMEM((modes, 2, 8, length), f32),
            pltpu.VMEM((8, length), f32),
            pltpu.VMEM((modes, 8, length), f32),
        ],
        compiler_params=pltpu.CompilerParams(vmem_limit_bytes=VMEM_BYTES),
        name="local_terms",
    )(positions, coeffs, gathered, object_field, following, intensities, *tables)
    object_step, probe_step = pl.pallas_call(
        functools.partial(reduce_kernel, scans, modes),
        out_shape=(
            jax.ShapeDtypeStruct(object_field.shape, f32),
            jax.ShapeDtypeStruct((2 * length, length), f32),
        ),
        in_specs=[vmem] * 2,
        out_specs=(vmem, vmem),
        scratch_shapes=[
            pltpu.VMEM((modes, length + EXTRA, length), f32),
            pltpu.VMEM((others, length + EXTRA, length), f32),
            pltpu.VMEM((groups, r1, b1 + EXTRA, length), f32),
            pltpu.VMEM((groups, max(r1 - 1, 1), b1 + EXTRA, length), f32),
            pltpu.VMEM((groups, r2, b2 + EXTRA, length), f32),
            pltpu.VMEM((groups, max(r2 - 1, 1), b2 + EXTRA, length), f32),
            pltpu.VMEM((EXTRA, length), f32),
            pltpu.VMEM((3, length, columns), f32),
            pltpu.VMEM((others, parts, 3, rows_c, columns), f32),
            pltpu.VMEM((others, parts, 3, rows_c, columns), f32),
            dma((groups,)), dma((groups,)),
            dma((groups, others)), dma((groups, others)),
            dma((groups, max(r1 - 1, 1))), dma((groups, max(r1 - 1, 1))),
            dma((groups, max(r2 - 1, 1))), dma((groups, max(r2 - 1, 1))),
            dma((groups, 1)), dma((groups, 1)),
            dma((groups, max(r1 - 1, 1))), dma((groups, max(r1 - 1, 1))),
            dma((groups, max(r2 - 1, 1))), dma((groups, max(r2 - 1, 1))),
            dma((modes, parts)), dma((modes, parts)),
            dma((others, parts)), dma((others, parts)),
            dma((others, parts)), dma((others, parts)),
        ],
        compiler_params=pltpu.CompilerParams(
            collective_id=1, has_side_effects=True, vmem_limit_bytes=VMEM_BYTES),
        name="reduce_terms",
    )(terms, grads)
    probes_new = eigen_probes + probe_step.reshape(eigen_probes.shape)
    return object_field + object_step, probes_new, coeffs_new


def solution(mesh):
    return jax.shard_map(
        functools.partial(on_device, mesh.shape["scan"], mesh.shape["mode"]),
        mesh=mesh,
        in_specs=(
            P(None, "scan", None),
            P("mode", None, None, None),
            P(("scan", "mode"), None, None),
            P(("scan", "mode"), None, None),
            P(("scan", "mode"), None),
        ),
        out_specs=(
            P(None, "scan", None),
            P("mode", None, None, None),
            P(("scan", "mode"), None, None),
        ),
        check_vma=False,
    )
```

```python
import functools
import math

import jax
import jax.numpy as jnp
import ml_dtypes
import numpy as np
from jax import lax
from jax.experimental import pallas as pl
from jax.experimental.pallas import tpu as pltpu
from jax.sharding import PartitionSpec as P

MAGNITUDE_FLOOR = 0.5
OBJECT_REGULARIZER = 1.0
EPSILON = 1e-05
MESH = pl.DeviceIdType.MESH
BLOCK = 64
EXTRA = 8
VMEM_BYTES = 56 * 1024 * 1024


def dft_tables(length):
    indices = np.arange(length)
    angle = (indices[:, None] * indices[None, :] % length) * (2.0 * math.pi / length)
    cosine = np.cos(angle) / math.sqrt(length)
    sine = -np.sin(angle) / math.sqrt(length)
    right = np.block([[cosine, sine], [-sine, cosine]])
    left = np.block([[cosine, -sine], [sine, cosine]])
    found = []
    for table in (right, left):
        high = table.astype(ml_dtypes.bfloat16)
        low = (table - high.astype(np.float64)).astype(ml_dtypes.bfloat16)
        found += [high, low]
    return found


def radices(count):
    rest = count // 2
    first = 1
    while first * first * 4 <= rest:
        first *= 2
    return first, rest // first


def gather_kernel(scans, modes, probe_ref, object_ref, gathered_ref, next_ref, *sems):
    send_y, recv_y, send_c, recv_c, send_o, recv_o = sems
    s = lax.axis_index("scan")
    m = lax.axis_index("mode")
    half = probe_ref.shape[0] // 2
    core = lax.rem(s, 2)
    sibling = s + 1 - 2 * core
    rows = pl.ds(pl.multiple_of(core * half, half), half)
    barrier = pltpu.get_barrier_semaphore()
    pl.semaphore_signal(barrier, inc=1, device_id=(sibling, m), device_id_type=MESH)
    for step in range(1, modes):
        other = lax.rem(m + step, modes)
        pl.semaphore_signal(barrier, inc=1, device_id=(s, other), device_id_type=MESH)

    @pl.when(s > 0)
    def _():
        pl.semaphore_signal(barrier, inc=1, device_id=(s - 1, m), device_id_type=MESH)

    @pl.when(s < scans - 1)
    def _():
        pl.semaphore_signal(barrier, inc=1, device_id=(s + 1, m), device_id_type=MESH)

    inner = jnp.minimum(s, 1) + jnp.minimum(scans - 1 - s, 1)
    pl.semaphore_wait(barrier, modes + inner)

    def object_copy(target):
        return pltpu.make_async_remote_copy(
            src_ref=object_ref, dst_ref=next_ref, send_sem=send_o, recv_sem=recv_o,
            device_id=(target, m), device_id_type=MESH)

    def mode_copy(step):
        return pltpu.make_async_remote_copy(
            src_ref=probe_ref.at[rows], dst_ref=gathered_ref.at[m, rows],
            send_sem=send_y.at[step - 1], recv_sem=recv_y.at[step - 1],
            device_id=(s, lax.rem(m + step, modes)), device_id_type=MESH)

    def sibling_copy(step):
        source = lax.rem(m + modes - step, modes)
        return pltpu.make_async_remote_copy(
            src_ref=gathered_ref.at[source, rows], dst_ref=gathered_ref.at[source, rows],
            send_sem=send_c.at[step - 1], recv_sem=recv_c.at[step - 1],
            device_id=(sibling, m), device_id_type=MESH)

    @pl.when(s > 0)
    def _():
        object_copy(s - 1).start()

    for step in range(1, modes):
        mode_copy(step).start()

    gathered_ref[m] = probe_ref[...]
    for step in range(1, modes):
        mode_copy(step).wait_recv()
        sibling_copy(step).start()
    for step in range(1, modes):
        mode_copy(step).wait_send()
        sibling_copy(step).wait_send()
        sibling_copy(step).wait_recv()

    @pl.when(s > 0)
    def _():
        object_copy(s - 1).wait_send()

    @pl.when(s < scans - 1)
    def _():
        object_copy(s + 1).wait_recv()


def compute_kernel(modes, place_ref, coef_ref, probe_ref, own_ref, next_ref, inten_ref,
                   rh_ref, rl_ref, lh_ref, ll_ref, terms_ref, grad_ref, coef_out_ref,
                   ext_ref, wave_ref, window_ref, mixed_ref, flat_ref, tall_ref, out_ref,
                   inner_ref, weight_ref, norm_ref):
    count, length = inten_ref.shape[0], inten_ref.shape[1]
    columns = own_ref.shape[2]
    blocks = length // BLOCK
    ext_ref[:, :length] = own_ref[...]
    ext_ref[:, length:] = next_ref[...]
    terms_ref[...] = jnp.zeros_like(terms_ref)
    grad_ref[...] = jnp.zeros_like(grad_ref)

    def folded(value):
        return jnp.sum(value.reshape(BLOCK // 8, 8, length), axis=0)

    def split(value):
        high = value.astype(jnp.bfloat16)
        return high, (value - high.astype(jnp.float32)).astype(jnp.bfloat16)

    def put_flat(rows, real, imag):
        for slot, value in enumerate((real, imag)):
            high, low = split(value)
            flat_ref[rows, slot * length:(slot + 1) * length] = high
            flat_ref[rows, (2 + slot) * length:(3 + slot) * length] = low

    def dot(a, b):
        return jnp.dot(a, b, preferred_element_type=jnp.float32)

    def right_apply(high_ref, low_ref):
        size = length // 2
        for start in range(0, length, size):
            rows = slice(start, start + size)
            for slot in range(2):
                cols = slice(slot * length, (slot + 1) * length)
                part = dot(
                    jnp.concatenate([flat_ref[rows, :], flat_ref[rows, :2 * length]], axis=1),
                    jnp.concatenate([high_ref[:, cols], high_ref[:, cols], low_ref[:, cols]], axis=0))
                part_high, part_low = split(part)
                base = slot * length + start
                tall_ref[base:base + size] = part_high
                tall_ref[base + 2 * length:base + 2 * length + size] = part_low

    def left_apply(high_ref, low_ref):
        size = length // 2
        for start in range(0, 2 * length, size):
            rows = slice(start, start + size)
            out_ref[rows] = dot(
                jnp.concatenate([high_ref[rows], high_ref[rows], low_ref[rows]], axis=1),
                jnp.concatenate([tall_ref[...], tall_ref[:2 * length]], axis=0))

    norm_ref[...] = jnp.zeros_like(norm_ref)

    def norms(index, carry):
        for mode in range(modes):
            rows = pl.ds(pl.multiple_of(index * BLOCK, BLOCK), BLOCK)
            value = probe_ref[mode, rows]
            norm_ref[mode] += folded(value * value)
        return carry

    lax.fori_loop(0, 2 * blocks, norms, 0)

    def pattern(b, carry):
        top = place_ref[b, 0] - lax.axis_index("scan") * length
        left = place_ref[b, 1]
        back_shift = lax.rem(columns - left, columns)
        within = lax.rem(top, 8)
        top_tile = top - within
        up_shift = lax.rem(8 - within, 8)
        sublane = lax.broadcasted_iota(jnp.int32, (BLOCK // 8, 8, length), 1)
        wide = lax.broadcasted_iota(jnp.int32, (BLOCK // 8 + 1, 8, columns), 1)
        inner_ref[...] = jnp.zeros_like(inner_ref)
        weight_ref[...] = jnp.zeros_like(weight_ref)

        def first(index, carry):
            base = pl.multiple_of(index * BLOCK, BLOCK)
            rows = pl.ds(base, BLOCK)
            lower = pl.ds(pl.multiple_of(base + length, BLOCK), BLOCK)
            pr = jnp.zeros((BLOCK, length), jnp.float32)
            pi = jnp.zeros((BLOCK, length), jnp.float32)
            for mode in range(modes):
                cr, ci = coef_ref[b, 0, mode], coef_ref[b, 1, mode]
                ur, ui = probe_ref[mode, rows], probe_ref[mode, lower]
                pr = pr + cr * ur - ci * ui
                pi = pi + cr * ui + ci * ur
            window = []
            for part in range(2):
                strip = ext_ref[part, pl.ds(pl.multiple_of(top_tile + base, 8), BLOCK + 8), :]
                strip = pltpu.roll(strip, back_shift, 1)[:, :length]
                turned = pltpu.roll(strip.reshape(BLOCK // 8 + 1, 8, length), up_shift, 1)
                kept = jnp.where(sublane < 8 - within, turned[:-1], turned[1:])
                window.append(kept.reshape(BLOCK, length))
            wr, wi = window
            window_ref[rows], window_ref[lower] = wr, wi
            mixed_ref[rows], mixed_ref[lower] = pr, pi
            weight_ref[...] += folded(wr * wr + wi * wi)
            real = pr * wr - pi * wi
            imag = pr * wi + pi * wr
            wave_ref[rows], wave_ref[lower] = real, imag
            put_flat(rows, real, imag)
            return carry

        lax.fori_loop(0, blocks, first, 0)
        right_apply(rh_ref, rl_ref)
        left_apply(lh_ref, ll_ref)

        def second(index, carry):
            base = pl.multiple_of(index * BLOCK, BLOCK)
            rows = pl.ds(base, BLOCK)
            lower = pl.ds(pl.multiple_of(base + length, BLOCK), BLOCK)
            real, imag = out_ref[rows], out_ref[lower]
            power = jnp.maximum(real * real + imag * imag, MAGNITUDE_FLOOR * MAGNITUDE_FLOOR)
            factor = jnp.sqrt(inten_ref[b, rows] / power)
            put_flat(rows, real * factor, imag * factor)
            return carry

        lax.fori_loop(0, blocks, second, 0)
        right_apply(lh_ref, ll_ref)
        left_apply(rh_ref, rl_ref)

        def third(index, carry):
            base = pl.multiple_of(index * BLOCK, BLOCK)
            rows = pl.ds(base, BLOCK)
            lower = pl.ds(pl.multiple_of(base + length, BLOCK), BLOCK)
            dr = out_ref[rows] - wave_ref[rows]
            di = out_ref[lower] - wave_ref[lower]
            pr, pi = mixed_ref[rows], mixed_ref[lower]
            wr, wi = window_ref[rows], window_ref[lower]
            pieces = (pr * dr + pi * di, pr * di - pi * dr, pr * pr + pi * pi)
            for part, piece in enumerate(pieces):
                padded = jnp.concatenate(
                    [piece, jnp.zeros((BLOCK, columns - length), jnp.float32)], axis=1)
                padded = pltpu.roll(padded, left, 1).reshape(BLOCK // 8, 8, columns)
                padded = pltpu.roll(padded, within, 1)
                edge = jnp.zeros((1, 8, columns), jnp.float32)
                placed = jnp.where(
                    wide >= within,
                    jnp.concatenate([padded, edge], axis=0),
                    jnp.concatenate([edge, padded], axis=0))
                spot = pl.ds(pl.multiple_of(top_tile + base, 8), BLOCK + 8)
                terms_ref[part, spot, :] += placed.reshape(BLOCK + 8, columns)
            gr = wr * dr + wi * di
            gi = wr * di - wi * dr
            for mode in range(modes):
                cr, ci = coef_ref[b, 0, mode], coef_ref[b, 1, mode]
                ur, ui = probe_ref[mode, rows], probe_ref[mode, lower]
                shifted = pl.ds(pl.multiple_of(base + EXTRA, 8), BLOCK)
                grad_ref[0, mode, shifted] += cr * gr + ci * gi
                grad_ref[1, mode, shifted] += cr * gi - ci * gr
                inner_ref[mode, 0] += folded(ur * gr + ui * gi)
                inner_ref[mode, 1] += folded(ur * gi - ui * gr)
            return carry

        lax.fori_loop(0, blocks, third, 0)

        def total(value):
            return jnp.sum(jnp.sum(value, axis=1, keepdims=True), axis=0, keepdims=True)

        weight = total(weight_ref[...]) * (1.0 / (length * length))
        lanes = lax.broadcasted_iota(jnp.int32, (1, modes), 1)
        found = [jnp.zeros((1, modes), jnp.float32)] * 2
        for mode in range(modes):
            cr, ci = coef_ref[b, 0, mode], coef_ref[b, 1, mode]
            denominator = total(norm_ref[mode]) * weight + EPSILON
            for part, c in enumerate((cr, ci)):
                value = c + total(inner_ref[mode, part]) / denominator
                found[part] = jnp.where(lanes == mode, value, found[part])
            share = jnp.broadcast_to((cr * cr + ci * ci) * weight, (1, length))
            for part in range(2):
                grad_ref[part, mode, :EXTRA] += jnp.broadcast_to(share, (EXTRA, length))
        coef_out_ref[b] = jnp.concatenate(found, axis=0)
        return carry

    lax.fori_loop(0, count, pattern, 0)


def reduce_kernel(scans, modes, terms_ref, grad_ref,
                  object_out_ref, probe_out_ref,
                  core_in, mode_in, stage1, in1, stage2, in2, weight_ref, shift_in, stage_n, numer_in,
                  send_g, recv_g, send_y, recv_y, send_1, recv_1, send_2, recv_2,
                  back_s0, back_r0, back_s1, back_r1, back_s2, back_r2,
                  send_s, recv_s, send_n, recv_n, send_a, recv_a):
    s = lax.axis_index("scan")
    m = lax.axis_index("mode")
    r1, r2 = radices(scans)
    length = terms_ref.shape[1] // 2
    d0 = lax.rem(s, 2)
    d1 = lax.rem(s // 2, r1)
    d2 = s // (2 * r1)
    rows_m = length // modes
    sibling = (s + 1 - 2 * d0, m)

    def peer1(step):
        return ((d2 * r1 + lax.rem(d1 + step, r1)) * 2 + d0, m)

    def peer2(step):
        return ((lax.rem(d2 + step, r2) * r1 + d1) * 2 + d0, m)

    def peer_m(step):
        return (s, lax.rem(m + step, modes))

    peers = [sibling] + [peer1(i) for i in range(1, r1)] + [peer2(i) for i in range(1, r2)]
    peers += [peer_m(i) for i in range(1, modes)]
    barrier = pltpu.get_barrier_semaphore()
    for peer in peers:
        pl.semaphore_signal(barrier, inc=1, device_id=peer, device_id_type=MESH)

    @pl.when(s > 0)
    def _():
        pl.semaphore_signal(barrier, inc=1, device_id=(s - 1, m), device_id_type=MESH)

    @pl.when(s < scans - 1)
    def _():
        pl.semaphore_signal(barrier, inc=1, device_id=(s + 1, m), device_id_type=MESH)

    inner = jnp.minimum(s, 1) + jnp.minimum(scans - 1 - s, 1)
    pl.semaphore_wait(barrier, len(peers) + inner)

    def remote(src, dst, send, recv, peer):
        return pltpu.make_async_remote_copy(
            src_ref=src, dst_ref=dst, send_sem=send, recv_sem=recv,
            device_id=peer, device_id_type=MESH)

    parts = send_s.shape[1]
    rows_c = rows_m // parts
    pending = []

    def begin(*arguments):
        copy = remote(*arguments)
        copy.start()
        pending.append(copy)
        return copy

    def chunk(owner, part):
        return pl.ds(pl.multiple_of(owner * rows_m + part * rows_c, rows_c), rows_c)

    def shift_copy(step, part, target):
        rows = chunk(lax.rem(m + step, modes), part)
        away = chunk(lax.rem(m + step, modes) + modes, part)
        return remote(terms_ref.at[:, away], shift_in.at[:, rows],
                      send_s.at[step - 1, part], recv_s.at[step - 1, part], (target, m))

    def shift_start(steps):
        @pl.when(s < scans - 1)
        def _():
            for step in steps:
                for part in range(parts):
                    shift_copy(step, part, s + 1).start()

    def shift_wait(step, part):
        @pl.when(s > 0)
        def _():
            shift_copy(step, part, s - 1).wait_recv()

    def gradient(q):
        size = length // groups
        extra = EXTRA if q == 0 else 0
        rows = pl.ds(0 if q == 0 else EXTRA + q * size, size + extra)
        c1, c2 = size // r1, size // (r1 * r2)
        core = begin(grad_ref.at[1 - d0, :, rows], core_in.at[:, rows],
                     send_g.at[q], recv_g.at[q], sibling)
        yield
        core.wait_recv()
        copies = []
        for step in range(1, modes):
            owner = lax.rem(m + step, modes)
            core_in[owner, rows] = core_in[owner, rows] + grad_ref[d0, owner, rows]
            copies.append(begin(core_in.at[owner, rows], mode_in.at[step - 1, rows],
                                send_y.at[q, step - 1], recv_y.at[q, step - 1], peer_m(step)))
        yield
        total = core_in[m, rows] + grad_ref[d0, m, rows]
        for step in range(1, modes):
            copies[step - 1].wait_recv()
            total = total + mode_in[step - 1, rows]
        levels = ((r1, c1, d1, stage1, in1, send_1, recv_1, peer1),
                  (r2, c2, d2, stage2, in2, send_2, recv_2, peer2))
        for radix, c, digit, stage, landed, send, recv, peer in levels:
            for index in range(radix):
                if extra:
                    stage[q, index, :extra] = total[:extra]
                stage[q, index, extra:extra + c] = total[extra + index * c:extra + (index + 1) * c]
            held = pl.ds(0, c + extra)
            copies = []
            for step in range(1, radix):
                copies.append(begin(stage.at[q, lax.rem(digit + step, radix), held],
                                    landed.at[q, step - 1, held],
                                    send.at[q, step - 1], recv.at[q, step - 1], peer(step)))
            yield
            total = stage[q, digit, held]
            for step in range(1, radix):
                copies[step - 1].wait_recv()
                total = total + landed[q, step - 1, held]
        if extra:
            weight_ref[...] = total[:extra]
        start0 = d0 * length + q * size
        start1 = start0 + d1 * c1
        start2 = start1 + d2 * c2
        block0 = pl.ds(pl.multiple_of(start0, size), size)
        block1 = pl.ds(pl.multiple_of(start1, c1), c1)
        block2 = pl.ds(pl.multiple_of(start2, c2), c2)
        probe_out_ref[block2] = total[extra:] / weight_ref[0:1]
        for block, radix, send, recv, peer in ((block2, r2, back_s2, back_r2, peer2),
                                               (block1, r1, back_s1, back_r1, peer1),
                                               (block0, 2, back_s0, back_r0, lambda step: sibling)):
            copies = []
            for step in range(1, radix):
                copies.append(begin(probe_out_ref.at[block], probe_out_ref.at[block],
                                    send.at[q, step - 1], recv.at[q, step - 1], peer(step)))
            yield
            for copy in copies:
                copy.wait_recv()
        yield

    def terms():
        copies = {}
        for part in range(parts):
            for step in range(1, modes):
                rows = chunk(lax.rem(m + step, modes), part)
                shift_wait(step, part)
                stage_n[step - 1, part] = terms_ref[:, rows] + shift_in[:, rows]
                copies[step, part] = begin(
                    stage_n.at[step - 1, part], numer_in.at[step - 1, part],
                    send_n.at[step - 1, part], recv_n.at[step - 1, part], peer_m(step))
            if part == parts - 1:
                shift_start([modes])
            yield
        back = []
        for part in range(parts):
            rows = chunk(m, part)
            shift_wait(modes, part)
            found = [terms_ref[k, rows] + shift_in[k, rows] for k in range(3)]
            for step in range(1, modes):
                copies[step, part].wait_recv()
                found = [found[k] + numer_in[step - 1, part, k] for k in range(3)]
            scale = found[2] + OBJECT_REGULARIZER
            for k in range(2):
                object_out_ref[k, rows] = found[k] / scale
            for step in range(1, modes):
                back.append(begin(object_out_ref.at[:, rows], object_out_ref.at[:, rows],
                                  send_a.at[step - 1, part], recv_a.at[step - 1, part], peer_m(step)))
            yield
        for copy in back:
            copy.wait_recv()
        yield

    groups = send_g.shape[0]
    chains = [gradient(q) for q in range(groups)]
    objects = terms()

    def advance():
        for chain in chains:
            next(chain)

    advance()
    shift_start(range(1, modes))

    @pl.when(s == 0)
    def _():
        shift_in[...] = jnp.zeros_like(shift_in)

    advance()
    next(objects)
    next(chains[0])
    for _ in range(parts - 1):
        next(objects)
    for chain in chains[1:]:
        next(chain)
    advance()
    for index in range(parts):
        next(objects)
        if index < 2:
            advance()
    for _ in range(2 - min(parts, 2)):
        advance()
    advance()
    advance()
    next(objects)

    @pl.when(s < scans - 1)
    def _():
        for step in range(1, modes + 1):
            for part in range(parts):
                shift_copy(step, part, s + 1).wait_send()

    for copy in pending:
        copy.wait_send()


def on_device(scans, modes, object_field, eigen_probes, coeffs, intensities, positions):
    length = eigen_probes.shape[2]
    columns = object_field.shape[2]
    f32 = jnp.float32
    vmem = pl.BlockSpec(memory_space=pltpu.VMEM)
    smem = pl.BlockSpec(memory_space=pltpu.SMEM)
    dma = pltpu.SemaphoreType.DMA
    probe = eigen_probes.reshape(2 * length, length)
    others = max(modes - 1, 1)
    r1, r2 = radices(scans)
    groups = 2 if length // (r1 * r2) >= 16 else 1
    b1, b2 = length // (r1 * groups), length // (r1 * r2 * groups)
    parts = 4 if modes == 2 else 1
    rows_c = length // (modes * parts)
    gathered, following = pl.pallas_call(
        functools.partial(gather_kernel, scans, modes),
        out_shape=(
            jax.ShapeDtypeStruct((modes, 2 * length, length), f32),
            jax.ShapeDtypeStruct(object_field.shape, f32),
        ),
        in_specs=[vmem] * 2,
        out_specs=(vmem, vmem),
        scratch_shapes=[dma((others,))] * 4 + [dma, dma],
        compiler_params=pltpu.CompilerParams(
            collective_id=0, has_side_effects=True, vmem_limit_bytes=VMEM_BYTES),
        name="gather_probes",
    )(probe, object_field)
    tables = [jnp.asarray(table) for table in dft_tables(length)]
    terms, grads, coeffs_new = pl.pallas_call(
        functools.partial(compute_kernel, modes),
        out_shape=(
            jax.ShapeDtypeStruct((3, 2 * length, columns), f32),
            jax.ShapeDtypeStruct((2, modes, length + EXTRA, length), f32),
            jax.ShapeDtypeStruct(coeffs.shape, f32),
        ),
        in_specs=[smem, smem] + [vmem] * 8,
        out_specs=(vmem, vmem, vmem),
        scratch_shapes=[
            pltpu.VMEM((2, 2 * length, columns), f32),
            pltpu.VMEM((2 * length, length), f32),
            pltpu.VMEM((2 * length, length), f32),
            pltpu.VMEM((2 * length, length), f32),
            pltpu.VMEM((length, 4 * length), jnp.bfloat16),
            pltpu.VMEM((4 * length, length), jnp.bfloat16),
            pltpu.VMEM((2 * length, length), f32),
            pltpu.VMEM((modes, 2, 8, length), f32),
            pltpu.VMEM((8, length), f32),
            pltpu.VMEM((modes, 8, length), f32),
        ],
        compiler_params=pltpu.CompilerParams(vmem_limit_bytes=VMEM_BYTES),
        name="local_terms",
    )(positions, coeffs, gathered, object_field, following, intensities, *tables)
    object_step, probe_step = pl.pallas_call(
        functools.partial(reduce_kernel, scans, modes),
        out_shape=(
            jax.ShapeDtypeStruct(object_field.shape, f32),
            jax.ShapeDtypeStruct((2 * length, length), f32),
        ),
        in_specs=[vmem] * 2,
        out_specs=(vmem, vmem),
        scratch_shapes=[
            pltpu.VMEM((modes, length + EXTRA, length), f32),
            pltpu.VMEM((others, length + EXTRA, length), f32),
            pltpu.VMEM((groups, r1, b1 + EXTRA, length), f32),
            pltpu.VMEM((groups, max(r1 - 1, 1), b1 + EXTRA, length), f32),
            pltpu.VMEM((groups, r2, b2 + EXTRA, length), f32),
            pltpu.VMEM((groups, max(r2 - 1, 1), b2 + EXTRA, length), f32),
            pltpu.VMEM((EXTRA, length), f32),
            pltpu.VMEM((3, length, columns), f32),
            pltpu.VMEM((others, parts, 3, rows_c, columns), f32),
            pltpu.VMEM((others, parts, 3, rows_c, columns), f32),
            dma((groups,)), dma((groups,)),
            dma((groups, others)), dma((groups, others)),
            dma((groups, max(r1 - 1, 1))), dma((groups, max(r1 - 1, 1))),
            dma((groups, max(r2 - 1, 1))), dma((groups, max(r2 - 1, 1))),
            dma((groups, 1)), dma((groups, 1)),
            dma((groups, max(r1 - 1, 1))), dma((groups, max(r1 - 1, 1))),
            dma((groups, max(r2 - 1, 1))), dma((groups, max(r2 - 1, 1))),
            dma((modes, parts)), dma((modes, parts)),
            dma((others, parts)), dma((others, parts)),
            dma((others, parts)), dma((others, parts)),
        ],
        compiler_params=pltpu.CompilerParams(
            collective_id=1, has_side_effects=True, vmem_limit_bytes=VMEM_BYTES),
        name="reduce_terms",
    )(terms, grads)
    probes_new = eigen_probes + probe_step.reshape(eigen_probes.shape)
    return object_field + object_step, probes_new, coeffs_new


def solution(mesh):
    return jax.shard_map(
        functools.partial(on_device, mesh.shape["scan"], mesh.shape["mode"]),
        mesh=mesh,
        in_specs=(
            P(None, "scan", None),
            P("mode", None, None, None),
            P(("scan", "mode"), None, None),
            P(("scan", "mode"), None, None),
            P(("scan", "mode"), None),
        ),
        out_specs=(
            P(None, "scan", None),
            P("mode", None, None, None),
            P(("scan", "mode"), None, None),
        ),
        check_vma=False,
    )
```
